256 devices in a mesh: req: 16 (over z_hi, x), mp: 16 (over z_lo, y, core).
Axes of the slice: x: 4, y: 4, z: 8 (z_hi: 4, z_lo: 2; z = z_hi * 2 + z_lo), core: 2. Of those that a mesh axis runs over, the one named last changes fastest.
Arguments:
- queries: bfloat16 [2048, 4096], P('req', 'mp'), may hold values from -6 to 6
- suffix_kv: bfloat16 [2, 2048, 4096], P(None, 'req', 'mp'), may hold values from -6 to 6
- prefix_kv: bfloat16 [2, 8192, 4096], P(None, 'req', 'mp'), may hold values from -6 to 6
- resid: bfloat16 [2048, 4096], P('req', 'mp'), may hold values from -6 to 6
- ln_gain: float32 [4096], replicated, may hold values from 0.1 to 1.9
- out_weight: bfloat16 [4096, 4096], P('mp'), may hold values from -0.125 to 0.125
- up_weight: bfloat16 [4096, 8192], P(None, 'mp'), may hold values from -0.09375 to 0.09375
- down_weight: bfloat16 [8192, 4096], P('mp'), may hold values from -0.09375 to 0.09375
- lengths: int32 [16], replicated, may hold values from 1 to 128, 1024 in all
- req_group: int32 [16], replicated, may hold values from 0 to 3, as said below
- prefix_owner: int32 [16], replicated, may hold values from 0 to 15, as said below
Outputs:
- attended: bfloat16 [2048, 4096], P('req', 'mp')
- layer_out: bfloat16 [2048, 4096], P('req', 'mp')
The draws below stay inside these ranges and needn't reach their ends.
Inputs may be any that keep to these rules, and one draw needn't show every extreme that they name: `req_group`: each of the 4 groups holds exactly 4 requests. `prefix_owner`: a permutation: every logical block is held by exactly one stored block.
All inputs are finite; a program needn't handle non-finite values.
Results may differ from the reference program's by a relative error of at most 0.029.
Values may be sent and summed in bfloat16 or wider, within the bound.
A program may use at most 128 MiB of HBM per device.

```python
import math
import jax
import jax.numpy as jnp
import numpy as np
from jax import lax

D = 4096
H = 32
DH = 128
FF = 8192
G = 4
KB = 512
S_MAX = 128
P_SIZE = 2048
REQUESTS = 16
N_MP = 16


def drawn_direction(key):
    return jax.random.rademacher(jax.random.fold_in(key, 9173), (DH,), dtype=jnp.float32)


def owner_table(key):
    block_total = G * P_SIZE // KB
    return jax.random.permutation(jax.random.fold_in(key, 61), jnp.arange(block_total, dtype=jnp.int32)).astype(jnp.int32)


def draw_prefix_owner(key, part):
    return owner_table(key)


def draw_queries(key, part):
    row_count = REQUESTS * S_MAX
    values = jax.random.normal(jax.random.fold_in(key, 11), (row_count, H, DH), jnp.float32)
    return jnp.clip(values, -6.0, 6.0).reshape(row_count, D).astype(jnp.bfloat16)


def draw_cache(key, salt_value, row_count):
    values = jax.random.normal(jax.random.fold_in(key, salt_value), (2, row_count, H, DH), jnp.float32)
    return jnp.clip(values, -6.0, 6.0)


def draw_suffix_kv(key, part):
    values = draw_cache(key, 23, REQUESTS * S_MAX)
    return values.reshape(2, REQUESTS * S_MAX, D).astype(jnp.bfloat16)


def draw_prefix_kv(key, part):
    row_count = G * P_SIZE
    values = draw_cache(key, 37, row_count)
    owners = owner_table(key)
    row_index = jnp.arange(row_count)
    first_block = owners[row_index // KB] % (P_SIZE // KB) == 0
    row_in = row_index % KB
    sink_strength = jnp.where(row_in == 1, 6.0, 5.9375)
    is_sink = first_block & ((row_in == 1) | (row_in == 2))
    sunk = jnp.where(is_sink[:, None, None], sink_strength[:, None, None] * drawn_direction(key)[None, None, :], values[0])
    values = jnp.stack([sunk, values[1]], axis=0)
    return jnp.clip(values, -6.0, 6.0).reshape(2, row_count, D).astype(jnp.bfloat16)


def draw_req_group(key, part):
    labels = jnp.arange(REQUESTS, dtype=jnp.int32) // (REQUESTS // G)
    return jax.random.permutation(jax.random.fold_in(key, 51), labels).astype(jnp.int32)


def spiked(array, key, source, target, blocks, factor):
    def block_of(axis_at):
        return (jnp.arange(array.shape[axis_at]) // (array.shape[axis_at] // blocks)).reshape((-1,) + (1,) * (array.ndim - 1 - axis_at))

    one_side = jax.random.permutation(key, blocks)[block_of(target)]
    far = (block_of(target) + blocks // 2) % blocks
    return jnp.where((block_of(source) == one_side) | (block_of(source) == far), factor * array, array)


def block_levels(rng, extent, pieces, least, high):
    gain = 1.0
    for position, shards_of in pieces:
        steps = jax.random.uniform(jax.random.fold_in(jax.random.fold_in(rng, 6), position), (shards_of,), jnp.float32, least / len(pieces), high / len(pieces))
        gain = gain * jnp.repeat(jnp.exp(steps), extent[position] // shards_of).reshape((-1,) + (1,) * (len(extent) - 1 - position))
    return gain


def length_profile(number_of, total, most, slope):
    weights = [(1 << 20) // math.isqrt(rank ** slope) + 1 for rank in range(2, number_of + 1)]
    spare, holding = total - most - (number_of - 1), [1] * (number_of - 1)
    while spare > 0:
        candidates = [i for i in range(number_of - 1) if holding[i] < most]
        pool, budget = sum([weights[i] for i in candidates]), spare
        for i in candidates:
            more = min(most - holding[i], max(1, budget * weights[i] // pool), spare)
            holding[i] = holding[i] + more
            spare = spare - more
    return np.array([most] + holding)


def uneven(stream_key, number_of, total, reach, slope):
    if number_of == 2:
        one = jax.random.randint(stream_key, (), max(1, total - reach), min(reach, total - 1) + 1)
        return jnp.stack([one, total - one])
    sizes = jnp.asarray(length_profile(number_of, total, reach, slope), jnp.int32)
    pairs = (number_of - 1) // 2
    giver, receiver = sizes[1:1 + 2 * pairs:2], sizes[2:2 + 2 * pairs:2]
    room = jnp.minimum(giver - 1, reach - receiver)
    shifted = jax.random.randint(jax.random.fold_in(stream_key, 1), (pairs,), 0, 1 << 20) % (room + 1)
    sizes = sizes.at[1:1 + 2 * pairs:2].set(giver - shifted).at[2:2 + 2 * pairs:2].set(receiver + shifted)
    return sizes[jax.random.permutation(jax.random.fold_in(stream_key, 2), number_of)]


def scatter_about(key, shape, spread, most, shards=(), kind=jnp.bfloat16):
    entries = jax.random.normal(key, shape, jnp.float32) * spread
    if len(shards) > 0:
        entries = block_levels(key, shape, shards, -0.22, 0.18) * entries
    return jnp.clip(entries, min=-most, max=most).astype(kind)


def heavy_noise(key, extent, width, bound, shards, heavy, kind=jnp.bfloat16):
    values = width * jax.random.normal(key, extent, jnp.float32)
    if shards:
        values = values * block_levels(key, extent, shards, -0.22, 0.18)
    return jnp.clip(spiked(values, jax.random.fold_in(key, 3), *heavy), -bound, bound).astype(kind)


def setup_inputs(seed: int = 0) -> dict:
    seeds = jax.random.split(jax.random.key(seed), 12)
    queries = draw_queries(jax.random.fold_in(seeds[11], 71), 0)
    suffix_kv = draw_suffix_kv(jax.random.fold_in(seeds[11], 71), 0)
    prefix_kv = draw_prefix_kv(jax.random.fold_in(seeds[11], 71), 0)
    resid = scatter_about(seeds[3], (REQUESTS * S_MAX, D), 1.0, 6.0, ((0, 16), (1, 16)))
    ln_gain = jnp.clip(1.0 + 0.18 * jax.random.normal(seeds[4], (D,), jnp.float32), 0.1, 1.9)
    out_weight = heavy_noise(seeds[5], (D, D), D ** -0.5, 0.125, ((0, 16),), (0, 1, 16, 2.0))
    up_weight = scatter_about(seeds[6], (D, FF), D ** -0.5, 0.09375, ((1, 16),))
    down_weight = heavy_noise(seeds[7], (FF, D), FF ** -0.5, 0.09375, ((0, 16),), (0, 1, 16, 2.0))
    lengths = uneven(seeds[8], REQUESTS, REQUESTS * S_MAX // 2, S_MAX, 2).astype(jnp.int32)
    req_group = draw_req_group(jax.random.fold_in(seeds[11], 71), 0)
    prefix_owner = draw_prefix_owner(jax.random.fold_in(seeds[11], 71), 0)
    return dict(queries=queries, suffix_kv=suffix_kv, prefix_kv=prefix_kv, resid=resid, ln_gain=ln_gain, out_weight=out_weight, up_weight=up_weight, down_weight=down_weight, lengths=lengths, req_group=req_group, prefix_owner=prefix_owner)


very_negative = -1e+30

def block_partial(query_rows, key_rows, value_rows, query_pos, key_pos, allowed, slopes, shared):
    if shared:
        score_form = 'rqhd,khd->rqhk'
        value_form = 'rqhk,khd->rqhd'
    else:
        score_form = 'rqhd,rkhd->rqhk'
        value_form = 'rqhk,rkhd->rqhd'
    scores = jnp.einsum(score_form, query_rows.astype(jnp.float32), key_rows.astype(jnp.float32)) * float(DH) ** (-0.5)
    distance = (query_pos[:, None, None] - key_pos[None, None, :]).astype(jnp.float32)
    scores = scores - slopes[None, :, None] * distance
    masked = jnp.where(allowed, scores, very_negative)
    maxima = lax.optimization_barrier(jnp.max(masked, axis=-1))
    weights = jnp.where(allowed, jnp.exp(masked - maxima[..., None]), 0.0)
    totals = lax.optimization_barrier(jnp.sum(weights, axis=-1))
    rounded = weights.astype(jnp.bfloat16)
    weighted = jnp.einsum(value_form, rounded.astype(jnp.float32), value_rows.astype(jnp.float32))
    return (weighted, maxima, totals)

def reference(queries, suffix_kv, prefix_kv, resid, ln_gain, out_weight, up_weight, down_weight, lengths, req_group, prefix_owner):
    row_count = queries.shape[0]
    req_count = row_count // S_MAX
    per_group = P_SIZE // KB
    stored = prefix_kv.reshape(2, G * per_group, KB, H, DH)
    logical = jnp.zeros_like(stored).at[:, prefix_owner].set(stored)
    head_ids = jnp.arange(H).astype(jnp.float32)
    slopes = jnp.power(2.0, -8.0 * (head_ids + 1.0) / H)
    query_all = queries.reshape(req_count, S_MAX, H, DH)
    suffix_all = suffix_kv.reshape(2, req_count, S_MAX, H, DH)
    offsets = jnp.arange(S_MAX).astype(jnp.int32)
    query_pos = P_SIZE + offsets

    def attend(req_index):
        req_len = lengths[req_index]
        group_id = req_group[req_index]
        my_query = query_all[req_index][None]
        allowed = (offsets[None, :] <= offsets[:, None]) & (offsets[None, :] < req_len)
        own_part = block_partial(my_query, suffix_all[0, req_index][None], suffix_all[1, req_index][None], query_pos, query_pos, allowed[None, :, None, :], slopes, False)
        group_blocks = lax.dynamic_slice_in_dim(logical, (group_id * per_group).astype(jnp.int32), per_group, 1)

        def prefix_part(block_index):
            key_pos = (block_index * KB + jnp.arange(KB)).astype(jnp.int32)
            return block_partial(my_query, group_blocks[0, block_index], group_blocks[1, block_index], query_pos, key_pos, True, slopes, True)
        parts = lax.map(prefix_part, jnp.arange(per_group).astype(jnp.int32))
        peak_max = jnp.maximum(own_part[1], lax.optimization_barrier(jnp.max(parts[1], axis=0)))
        own_scale = jnp.exp(own_part[1] - peak_max)
        part_scale = jnp.exp(parts[1] - peak_max[None])
        numerator = own_part[0] * own_scale[..., None] + lax.optimization_barrier(jnp.sum(parts[0] * part_scale[..., None], axis=0))
        denominator = own_part[2] * own_scale + lax.optimization_barrier(jnp.sum(parts[2] * part_scale, axis=0))
        outcome = (numerator / denominator[..., None])[0]
        live_mask = offsets < req_len
        return jnp.where(live_mask[:, None, None], outcome, 0.0).astype(jnp.bfloat16)
    attended = lax.map(attend, jnp.arange(req_count).astype(jnp.int32)).reshape(row_count, H * DH)
    columns = D // N_MP
    units = FF // N_MP
    residual = resid.astype(jnp.float32)
    mixed_rows = jnp.zeros((row_count, D), jnp.float32)
    for group_index in range(N_MP):
        low = group_index * columns
        head_term = jnp.dot(attended[:, low:low + columns], out_weight[low:low + columns, :], preferred_element_type=jnp.float32)
        head_term = head_term.at[:, low:low + columns].add(residual[:, low:low + columns])
        mixed_rows = mixed_rows + lax.optimization_barrier(head_term.astype(jnp.bfloat16)).astype(jnp.float32)
    row_mean = lax.optimization_barrier(jnp.mean(mixed_rows, axis=1, keepdims=True))
    centered = mixed_rows - row_mean
    variance = lax.optimization_barrier(jnp.mean(centered * centered, axis=1, keepdims=True))
    normed = (centered * lax.rsqrt(variance + 1e-05) * ln_gain).astype(jnp.bfloat16)
    hidden = jax.nn.gelu(jnp.dot(normed, up_weight, preferred_element_type=jnp.float32), approximate=False).astype(jnp.bfloat16)
    update = jnp.zeros((row_count, D), jnp.float32)
    for group_index in range(N_MP):
        low = group_index * units
        unit_term = jnp.dot(hidden[:, low:low + units], down_weight[low:low + units, :], preferred_element_type=jnp.float32)
        update = update + lax.optimization_barrier(unit_term.astype(jnp.bfloat16)).astype(jnp.float32)
    live_rows = jnp.arange(row_count) % S_MAX < jnp.repeat(lengths, S_MAX)
    layer_out = jnp.where(live_rows[:, None], mixed_rows + update, 0.0).astype(jnp.bfloat16)
    return (attended, layer_out)
```

```python
import functools

import jax
import jax.numpy as jnp
from jax import lax
from jax.experimental import pallas as pl
from jax.experimental.pallas import tpu as pltpu
from jax.sharding import PartitionSpec as P

MESH = pl.DeviceIdType.MESH
H = 32
DH = 128
KB = 512
S_MAX = 128
P_SIZE = 2048
PER_GROUP = P_SIZE // KB
NX = 4
NZH = 4
NY = 4
NZL = 2
NCHIP = NY * NZL
NREQ = NX * NZH
NEG = -1e30
ROWS = S_MAX
COLS = 2 * DH
D = 4096
HALF = D // 2
UNITS = 512
STAT = 16
SLOT = COLS + STAT

Z_FAR = (2, 1, 3)
X_NEAR = (1, 3, 2)
CHIPS = ((1, 2), (1, 1), (1, 3), (0, 2), (1, 0), (0, 1), (0, 3))

F32 = jnp.float32
BF16 = jnp.bfloat16


def nt(a, b):
    return lax.dot_general(a, b, (((1,), (1,)), ((), ())), preferred_element_type=F32)


def nn(a, b):
    return lax.dot_general(a, b, (((1,), (0,)), ((), ())), preferred_element_type=F32)


def slope_of(head):
    k = head + 1
    whole, part = k // 4, lax.rem(k, 4)
    out = jnp.float32(1.0)
    for i in range(1, 9):
        out = jnp.where(whole == i, jnp.float32(2.0**-i), out)
    frac = jnp.float32(1.0)
    for i in range(1, 4):
        frac = jnp.where(part == i, jnp.float32(2.0 ** (-0.25 * i)), frac)
    return out * frac


def split3(v):
    hi = v.astype(BF16).astype(F32)
    rest = v - hi
    mid = rest.astype(BF16).astype(F32)
    return hi, mid, rest - mid


def pack_stats(ms, ls):
    row = lax.broadcasted_iota(jnp.int32, (STAT, ROWS), 0)
    out = jnp.zeros((STAT, ROWS), F32)
    at = 0
    for m, l in zip(ms, ls):
        for part in split3(m) + split3(l):
            out = jnp.where(row == at, part, out)
            at += 1
    return out.astype(BF16)


def unpack_stats(block):
    st = block.astype(F32)
    ms, ls = [], []
    for h in range(2):
        at = 6 * h
        ms.append(st[at : at + 1] + st[at + 1 : at + 2] + st[at + 2 : at + 3])
        ls.append(st[at + 3 : at + 4] + st[at + 4 : at + 5] + st[at + 5 : at + 6])
    return ms, ls


def combine(parts):
    ms, ls, os = [], [], []
    for h in range(2):
        m = parts[0][0][h]
        for part in parts[1:]:
            m = jnp.maximum(m, part[0][h])
        l, o = None, None
        for part in parts:
            scale = jnp.exp(part[0][h] - m)
            pl_, po = part[1][h] * scale, part[2][h] * scale
            l = pl_ if l is None else l + pl_
            o = po if o is None else o + po
        ms.append(m)
        ls.append(l)
        os.append(o)
    return ms, ls, os


def read_slot(ref, lead):
    ms, ls = unpack_stats(ref[lead + (pl.ds(COLS, STAT), slice(None))])
    os = [ref[lead + (pl.ds(h * DH, DH), slice(None))].astype(F32) for h in range(2)]
    return ms, ls, os


def erf(x):
    return lax.erf(x)


def kernel(
    len_ref,
    grp_ref,
    own_ref,
    q_hbm,
    skv_hbm,
    pkv_hbm,
    res_hbm,
    gain_hbm,
    ow_hbm,
    uw_hbm,
    dw_hbm,
    att_out,
    lay_out,
    qall,
    qv,
    skv,
    pkv,
    res,
    gain,
    ow,
    uw,
    dw,
    vt,
    sufo,
    sufs,
    obuf,
    sendb,
    xrecv,
    zsend,
    zrecv,
    respad,
    pre_s,
    pre_r,
    rs_s,
    rs_r,
    st_s,
    st_r,
    mixed,
    nall,
    tmp,
    pre2_s,
    pre2_r,
    rs2_s,
    rs2_r,
    loc,
    qzs,
    qxs,
    qrs,
    pxs,
    pxr,
    pzs,
    pzr,
    p1s,
    p1r,
    r1s,
    r1r,
    sts,
    strv,
    ags,
    agr,
    fws,
    fwr,
    p2s,
    p2r,
    r2s,
    r2r,
):
    me_r = lax.axis_index("req")
    me_m = lax.axis_index("mp")
    zh, x = me_r // NX, lax.rem(me_r, NX)
    core = lax.rem(me_m, 2)
    chip = me_m // 2
    zl, y = chip // NY, lax.rem(chip, NY)
    other = 1 - core

    def req_at(dz, dx):
        return lax.rem(zh + dz, NZH) * NX + lax.rem(x + dx, NX)

    def req_dev(dz, dx):
        return (req_at(dz, dx), me_m)

    def chip_at(off):
        return lax.rem(zl + off[0], NZL) * NY + lax.rem(y + off[1], NY)

    def back(off):
        return lax.rem(zl + off[0], NZL) * NY + lax.rem(y + NY - off[1], NY)

    def chip_dev(off):
        return (me_r, chip_at(off) * 2 + core)

    partner = (me_r, chip * 2 + other)
    sends = []

    def send(src, dst, ssem, rsem, dev):
        cp = pltpu.make_async_remote_copy(
            src_ref=src, dst_ref=dst, send_sem=ssem, recv_sem=rsem, device_id=dev, device_id_type=MESH
        )
        cp.start()
        sends.append(cp)

    def arrive(dst, ssem, rsem):
        pltpu.make_async_remote_copy(
            src_ref=dst, dst_ref=dst, send_sem=ssem, recv_sem=rsem, device_id=partner, device_id_type=MESH
        ).wait_recv()

    loads = {}
    for i, (name, src, dst) in enumerate(
        (
            ("q", q_hbm, qv),
            ("qa", q_hbm, qall.at[me_r]),
            ("skv", skv_hbm, skv),
            ("pkv", pkv_hbm, pkv),
            ("res", res_hbm, res),
            ("gain", gain_hbm, gain),
            ("ow", ow_hbm, ow),
            ("uw", uw_hbm, uw),
            ("dw", dw_hbm, dw),
        )
    ):
        loads[name] = pltpu.make_async_copy(src, dst, loc.at[i])
        loads[name].start()

    barrier = pltpu.get_barrier_semaphore()
    peers = [req_dev(d, 0) for d in Z_FAR] + [req_dev(0, d) for d in X_NEAR]
    peers += [chip_dev(o) for o in CHIPS] + [partner]
    for dev in peers:
        pl.semaphore_signal(barrier, inc=1, device_id=dev, device_id_type=MESH)
    pl.semaphore_wait(barrier, len(peers))

    for i, d in enumerate(Z_FAR):
        send(q_hbm, qall.at[me_r], qzs.at[i], qrs.at[me_r], req_dev(d, 0))
    for i, d in enumerate(X_NEAR):
        send(q_hbm, qall.at[me_r], qxs.at[0, i], qrs.at[me_r], req_dev(0, d))

    my_len = len_ref[me_r]
    slopes = [slope_of(2 * me_m + h) for h in range(2)]
    scale = float(DH) ** (-0.5)
    loads["q"].wait()
    loads["skv"].wait()
    key_i = lax.broadcasted_iota(jnp.int32, (S_MAX, ROWS), 0)
    slot_i = lax.broadcasted_iota(jnp.int32, (S_MAX, ROWS), 1)
    allowed = (key_i <= slot_i) & (key_i < my_len)
    gap = (slot_i - key_i).astype(F32)
    for h in range(2):
        cols = slice(h * DH, (h + 1) * DH)
        s = nt(skv[0, :, cols], qv[:, cols]) * scale - slopes[h] * gap
        s = jnp.where(allowed, s, NEG)
        m = jnp.max(s, axis=0, keepdims=True)
        w = jnp.where(allowed, jnp.exp(s - m), 0.0)
        sufs[2 * h : 2 * h + 1, :] = m
        sufs[2 * h + 1 : 2 * h + 2, :] = jnp.sum(w, axis=0, keepdims=True)
        sufo[h] = nn(skv[1, :, cols].T, w.astype(BF16))
    loads["pkv"].wait()
    for h in range(2):
        vt[h] = pkv[1, :, h * DH : (h + 1) * DH].T

    for j, d in enumerate((1, 3, 2)):
        src = req_at(d, 0)
        arrive(qall.at[src], qzs.at[0], qrs.at[src])
        for i, dx in enumerate(X_NEAR):
            send(qall.at[src], qall.at[src], qxs.at[1 + j, i], qrs.at[src], req_dev(0, dx))

    logical = own_ref[me_r]
    group = logical // PER_GROUP
    base = (logical - group * PER_GROUP) * KB
    picks = [jnp.int32(0)] * 4
    sel = []
    seen = jnp.int32(0)
    for r in range(NREQ):
        hit = grp_ref[r] == group
        for j in range(4):
            picks[j] = jnp.where(hit & (seen == j), jnp.int32(r), picks[j])
        sel.append(jnp.where(hit, jnp.minimum(seen, 3), 4))
        seen = seen + jnp.where(hit, 1, 0)
    obuf[4] = jnp.concatenate(
        [
            jnp.zeros((COLS, ROWS), BF16),
            pack_stats([jnp.full((1, ROWS), NEG, F32)] * 2, [jnp.zeros((1, ROWS), F32)] * 2),
        ],
        axis=0,
    )

    loads["qa"].wait()
    for dz in (0, 1, 3, 2):
        for dx in X_NEAR:
            src = req_at(dz, dx)
            arrive(qall.at[src], qzs.at[0], qrs.at[src])

    pkey = lax.broadcasted_iota(jnp.int32, (KB, ROWS), 0)
    pslot = lax.broadcasted_iota(jnp.int32, (KB, ROWS), 1)
    dist = (P_SIZE - base + pslot - pkey).astype(F32)
    for j in range(4):
        ms, ls = [], []
        for h in range(2):
            cols = slice(h * DH, (h + 1) * DH)
            s = nt(pkv[0, :, cols], qall[picks[j], :, cols]) * scale - slopes[h] * dist
            m = jnp.max(s, axis=0, keepdims=True)
            w = jnp.exp(s - m)
            ms.append(m)
            ls.append(jnp.sum(w, axis=0, keepdims=True))
            obuf[j, cols, :] = nn(vt[h], w.astype(BF16)).astype(BF16)
        obuf[j, COLS:SLOT, :] = pack_stats(ms, ls)
    for r in range(NREQ):
        sendb[r] = obuf[sel[r]]

    for dz in (2, 1, 3, 0):
        for i, dx in enumerate(X_NEAR):
            send(sendb.at[req_at(dz, dx)], xrecv.at[dx - 1, dz], pxs.at[dx - 1, dz], pxr.at[dx - 1, dz], req_dev(0, dx))
    final = None
    for dz in (2, 1, 3, 0):
        parts = [read_slot(sendb, (req_at(dz, 0),))]
        for dx in X_NEAR:
            arrive(xrecv.at[dx - 1, dz], pxs.at[dx - 1, dz], pxr.at[dx - 1, dz])
            parts.append(read_slot(xrecv, (dx - 1, dz)))
        if dz == 0:
            parts.append(
                (
                    [sufs[0:1, :], sufs[2:3, :]],
                    [sufs[1:2, :], sufs[3:4, :]],
                    [sufo[0], sufo[1]],
                )
            )
        ms, ls, os = combine(parts)
        if dz == 0:
            final = (ms, ls, os)
        else:
            for h in range(2):
                zsend[dz - 1, h * DH : (h + 1) * DH, :] = os[h].astype(BF16)
            zsend[dz - 1, COLS:SLOT, :] = pack_stats(ms, ls)
            send(zsend.at[dz - 1], zrecv.at[dz - 1], pzs.at[dz - 1], pzr.at[dz - 1], req_dev(dz, 0))
    parts = [final]
    for dz in (1, 3, 2):
        arrive(zrecv.at[dz - 1], pzs.at[dz - 1], pzr.at[dz - 1])
        parts.append(read_slot(zrecv, (dz - 1,)))
    ms, ls, os = combine(parts)
    live = lax.broadcasted_iota(jnp.int32, (DH, ROWS), 1) < my_len
    for h in range(2):
        att_out[:, h * DH : (h + 1) * DH] = jnp.where(live, os[h] / ls[h], 0.0).T.astype(BF16)

    loads["res"].wait()
    loads["ow"].wait()
    respad[...] = jnp.zeros_like(respad)
    respad[:, pl.ds(pl.multiple_of(core * COLS, COLS), COLS)] = res[...].astype(F32)
    wide = 512

    def head_term(half, n):
        at = pl.multiple_of(half * HALF + n * wide, wide)
        t = nn(att_out[...], ow[:, pl.ds(at, wide)])
        return t + jnp.where(half * (HALF // wide) + n == chip, respad[...], 0.0)

    for n in range(HALF // wide):
        pre_s[n] = head_term(other, n).astype(BF16)
        send(pre_s.at[n], pre_r.at[n], p1s.at[n], p1r.at[n], partner)
    for n in range(HALF // wide):
        t = head_term(core, n)
        arrive(pre_r.at[n], p1s.at[n], p1r.at[n])
        rs_s[:, n * wide : (n + 1) * wide] = (t + pre_r[n].astype(F32)).astype(BF16)
    for i, off in enumerate(CHIPS):
        rows = pl.ds(pl.multiple_of(chip_at(off) * 16, 16), 16)
        send(rs_s.at[rows], rs_r.at[i], r1s.at[i], r1r.at[i], chip_dev(off))
    my_rows = pl.ds(pl.multiple_of(chip * 16, 16), 16)
    tot = rs_s[my_rows, :].astype(F32)
    for i in reversed(range(len(CHIPS))):
        arrive(rs_r.at[i], r1s.at[i], r1r.at[i])
        tot = tot + rs_r[i].astype(F32)

    mean_a = jnp.sum(tot, axis=1, keepdims=True) * (1.0 / HALF)
    cent = tot - mean_a
    m2_a = jnp.sum(cent * cent, axis=1, keepdims=True)
    lane = lax.broadcasted_iota(jnp.int32, (16, 128), 1)
    st_s[...] = jnp.where(lane < 64, mean_a, m2_a)
    send(st_s, st_r, sts.at[0], strv.at[0], partner)
    mixed[...] = tot
    loads["gain"].wait()
    arrive(st_r, sts.at[0], strv.at[0])
    mean_b, m2_b = st_r[:, 0:1], st_r[:, 64:65]
    diff = mean_a - mean_b
    mean = 0.5 * (mean_a + mean_b)
    var = (m2_a + m2_b + diff * diff * (HALF / 2)) * (1.0 / D)
    my_gain = gain[0:1, pl.ds(pl.multiple_of(core * HALF, HALF), HALF)]
    nall[core, my_rows, :] = ((tot - mean) * lax.rsqrt(var + 1e-05) * my_gain).astype(BF16)
    for i, off in enumerate(CHIPS):
        send(nall.at[core, my_rows], nall.at[core, my_rows], ags.at[i], agr.at[i], chip_dev(off))
    send(nall.at[core, my_rows], nall.at[core, my_rows], fws.at[7], fwr.at[7], partner)
    for i in reversed(range(len(CHIPS))):
        rows = pl.ds(pl.multiple_of(back(CHIPS[i]) * 16, 16), 16)
        arrive(nall.at[core, rows], ags.at[i], agr.at[i])
        send(nall.at[core, rows], nall.at[core, rows], fws.at[i], fwr.at[i], partner)

    loads["uw"].wait()
    acc = nn(nall[core], uw[pl.ds(pl.multiple_of(core * HALF, HALF), HALF), :])
    for i in range(len(CHIPS)):
        rows = pl.ds(pl.multiple_of(back(CHIPS[i]) * 16, 16), 16)
        arrive(nall.at[other, rows], fws.at[i], fwr.at[i])
    arrive(nall.at[other, my_rows], fws.at[7], fwr.at[7])
    acc = acc + nn(nall[other], uw[pl.ds(pl.multiple_of(other * HALF, HALF), HALF), :])
    hid = (acc * (0.5 * (1.0 + erf(acc * (0.5**0.5))))).astype(BF16)

    loads["dw"].wait()
    order = CHIPS + ((0, 0),)

    def unit_term(off, which):
        block = chip_at(off) * 2 + which
        t = nn(hid, dw[:, pl.ds(pl.multiple_of(block * COLS, COLS), COLS)])
        inner = lax.rem(block, NCHIP)
        add = mixed[:, pl.ds(pl.multiple_of(inner * COLS, COLS), COLS)]
        tmp[...] = t
        tmp[my_rows, :] = tmp[my_rows, :] + jnp.where(block // NCHIP == core, add, 0.0)
        return tmp[...]

    for i, off in enumerate(order):
        pre2_s[i] = unit_term(off, other).astype(BF16)
        send(pre2_s.at[i], pre2_r.at[i], p2s.at[i], p2r.at[i], partner)
    out = None
    for i, off in enumerate(order):
        t = unit_term(off, core)
        arrive(pre2_r.at[i], p2s.at[i], p2r.at[i])
        t = t + pre2_r[i].astype(F32)
        if i < len(CHIPS):
            rs2_s[i] = t.astype(BF16)
            send(rs2_s.at[i], rs2_r.at[i], r2s.at[i], r2r.at[i], chip_dev(off))
        else:
            out = t
    for i in reversed(range(len(CHIPS))):
        arrive(rs2_r.at[i], r2s.at[i], r2r.at[i])
        out = out + rs2_r[i].astype(F32)
    row_live = lax.broadcasted_iota(jnp.int32, (ROWS, COLS), 0) < my_len
    lay_out[...] = jnp.where(row_live, out, 0.0).astype(BF16)
    for cp in sends:
        cp.wait_send()


def shards(
    queries,
    suffix_kv,
    prefix_kv,
    resid,
    ln_gain,
    out_weight,
    up_weight,
    down_weight,
    lengths,
    req_group,
    prefix_owner,
):
    smem = pl.BlockSpec(memory_space=pltpu.SMEM)
    anym = pl.BlockSpec(memory_space=pl.ANY)
    vmem = pl.BlockSpec(memory_space=pltpu.VMEM)
    dma = pltpu.SemaphoreType.DMA
    vm = pltpu.VMEM
    n = HALF // 512
    nc = len(CHIPS)
    return pl.pallas_call(
        kernel,
        out_shape=[jax.ShapeDtypeStruct((ROWS, COLS), BF16)] * 2,
        in_specs=[smem] * 3 + [anym] * 8,
        out_specs=[vmem] * 2,
        scratch_shapes=[
            vm((NREQ, ROWS, COLS), BF16),
            vm((ROWS, COLS), BF16),
            vm((2, S_MAX, COLS), BF16),
            vm((2, KB, COLS), BF16),
            vm((ROWS, COLS), BF16),
            vm((1, D), F32),
            vm((COLS, D), BF16),
            vm((D, UNITS), BF16),
            vm((UNITS, D), BF16),
            vm((2, DH, KB), BF16),
            vm((2, DH, ROWS), F32),
            vm((8, ROWS), F32),
            vm((5, SLOT, ROWS), BF16),
            vm((NREQ, SLOT, ROWS), BF16),
            vm((3, NZH, SLOT, ROWS), BF16),
            vm((3, SLOT, ROWS), BF16),
            vm((3, SLOT, ROWS), BF16),
            vm((ROWS, 512), F32),
            vm((n, ROWS, 512), BF16),
            vm((n, ROWS, 512), BF16),
            vm((ROWS, HALF), BF16),
            vm((nc, 16, HALF), BF16),
            vm((16, 128), F32),
            vm((16, 128), F32),
            vm((16, HALF), F32),
            vm((2, ROWS, HALF), BF16),
            vm((ROWS, COLS), F32),
            vm((8, ROWS, COLS), BF16),
            vm((8, ROWS, COLS), BF16),
            vm((nc, ROWS, COLS), BF16),
            vm((nc, ROWS, COLS), BF16),
            dma((9,)),
            dma((3,)),
            dma((4, 3)),
            dma((NREQ,)),
            dma((3, NZH)),
            dma((3, NZH)),
            dma((3,)),
            dma((3,)),
            dma((n,)),
            dma((n,)),
            dma((nc,)),
            dma((nc,)),
            dma((1,)),
            dma((1,)),
            dma((nc,)),
            dma((nc,)),
            dma((8,)),
            dma((8,)),
            dma((8,)),
            dma((8,)),
            dma((nc,)),
            dma((nc,)),
        ],
        compiler_params=pltpu.CompilerParams(
            collective_id=0, has_side_effects=True, vmem_limit_bytes=56 * 2**20
        ),
        name="prefill_layer",
    )(
        lengths,
        req_group,
        prefix_owner,
        queries,
        suffix_kv,
        prefix_kv,
        resid,
        ln_gain.reshape(1, D),
        out_weight,
        up_weight,
        down_weight,
    )


def solution(mesh):
    placed = (
        P("req", "mp"),
        P(None, "req", "mp"),
        P(None, "req", "mp"),
        P("req", "mp"),
        P(),
        P("mp", None),
        P(None, "mp"),
        P("mp", None),
        P(),
        P(),
        P(),
    )
    return jax.shard_map(
        shards,
        mesh=mesh,
        in_specs=placed,
        out_specs=(P("req", "mp"), P("req", "mp")),
        check_vma=False,
    )
```

```python
import functools

import jax
import jax.numpy as jnp
from jax import lax
from jax.experimental import pallas as pl
from jax.experimental.pallas import tpu as pltpu
from jax.sharding import PartitionSpec as P

MESH = pl.DeviceIdType.MESH
H = 32
DH = 128
KB = 512
S_MAX = 128
P_SIZE = 2048
PER_GROUP = P_SIZE // KB
NX = 4
NZH = 4
NY = 4
NZL = 2
NCHIP = NY * NZL
NREQ = NX * NZH
NEG = -1e30
ROWS = S_MAX
COLS = 2 * DH
D = 4096
HALF = D // 2
UNITS = 512
STAT = 16
SLOT = COLS + STAT

Z_FAR = (2, 1, 3)
CHIPS = ((1, 2), (1, 1), (1, 3), (0, 2), (1, 0), (0, 1), (0, 3))

F32 = jnp.float32
BF16 = jnp.bfloat16


def nt(a, b):
    return lax.dot_general(a, b, (((1,), (1,)), ((), ())), preferred_element_type=F32)


def nn(a, b):
    return lax.dot_general(a, b, (((1,), (0,)), ((), ())), preferred_element_type=F32)


def slope_of(head):
    k = head + 1
    whole, part = k // 4, lax.rem(k, 4)
    out = jnp.float32(1.0)
    for i in range(1, 9):
        out = jnp.where(whole == i, jnp.float32(2.0**-i), out)
    frac = jnp.float32(1.0)
    for i in range(1, 4):
        frac = jnp.where(part == i, jnp.float32(2.0 ** (-0.25 * i)), frac)
    return out * frac


def split3(v):
    hi = v.astype(BF16).astype(F32)
    rest = v - hi
    mid = rest.astype(BF16).astype(F32)
    return hi, mid, rest - mid


def pack_stats(ms, ls):
    row = lax.broadcasted_iota(jnp.int32, (STAT, ROWS), 0)
    out = jnp.zeros((STAT, ROWS), F32)
    at = 0
    for m, l in zip(ms, ls):
        for part in split3(m) + split3(l):
            out = jnp.where(row == at, part, out)
            at += 1
    return out.astype(BF16)


def unpack_stats(block):
    st = block.astype(F32)
    ms, ls = [], []
    for h in range(2):
        at = 6 * h
        ms.append(st[at : at + 1] + st[at + 1 : at + 2] + st[at + 2 : at + 3])
        ls.append(st[at + 3 : at + 4] + st[at + 4 : at + 5] + st[at + 5 : at + 6])
    return ms, ls


def combine(parts):
    ms, ls, os = [], [], []
    for h in range(2):
        m = parts[0][0][h]
        for part in parts[1:]:
            m = jnp.maximum(m, part[0][h])
        l, o = None, None
        for part in parts:
            scale = jnp.exp(part[0][h] - m)
            pl_, po = part[1][h] * scale, part[2][h] * scale
            l = pl_ if l is None else l + pl_
            o = po if o is None else o + po
        ms.append(m)
        ls.append(l)
        os.append(o)
    return ms, ls, os


def read_slot(ref, lead):
    ms, ls = unpack_stats(ref[lead + (pl.ds(COLS, STAT), slice(None))])
    os = [ref[lead + (pl.ds(h * DH, DH), slice(None))].astype(F32) for h in range(2)]
    return ms, ls, os


def erf(x):
    return lax.erf(x)


def kernel(
    len_ref,
    grp_ref,
    own_ref,
    q_hbm,
    skv_hbm,
    pkv_hbm,
    res_hbm,
    gain_hbm,
    ow_hbm,
    uw_hbm,
    dw_hbm,
    att_out,
    lay_out,
    qz,
    skv,
    kvb,
    res,
    gain,
    ow,
    uw,
    dw,
    vt,
    sufo,
    sufs,
    acco,
    accs,
    zsend,
    zrecv,
    respad,
    pre_s,
    pre_r,
    rs_s,
    rs_r,
    st_s,
    st_r,
    mixed,
    nall,
    tmp,
    pre2_s,
    pre2_r,
    rs2_s,
    rs2_r,
    loc,
    qzs,
    qzr,
    kvs,
    kvr,
    pzs,
    pzr,
    p1s,
    p1r,
    r1s,
    r1r,
    sts,
    strv,
    ags,
    agr,
    fws,
    fwr,
    p2s,
    p2r,
    r2s,
    r2r,
):
    me_r = lax.axis_index("req")
    me_m = lax.axis_index("mp")
    zh, x = me_r // NX, lax.rem(me_r, NX)
    core = lax.rem(me_m, 2)
    chip = me_m // 2
    zl, y = chip // NY, lax.rem(chip, NY)
    other = 1 - core

    def req_at(dz, dx):
        return lax.rem(zh + dz, NZH) * NX + lax.rem(x + dx, NX)

    def req_dev(dz, dx):
        return (req_at(dz, dx), me_m)

    def chip_at(off):
        return lax.rem(zl + off[0], NZL) * NY + lax.rem(y + off[1], NY)

    def back(off):
        return lax.rem(zl + off[0], NZL) * NY + lax.rem(y + NY - off[1], NY)

    def chip_dev(off):
        return (me_r, chip_at(off) * 2 + core)

    partner = (me_r, chip * 2 + other)
    sends = []

    def send(src, dst, ssem, rsem, dev):
        cp = pltpu.make_async_remote_copy(
            src_ref=src, dst_ref=dst, send_sem=ssem, recv_sem=rsem, device_id=dev, device_id_type=MESH
        )
        cp.start()
        sends.append(cp)

    def arrive(dst, ssem, rsem):
        pltpu.make_async_remote_copy(
            src_ref=dst, dst_ref=dst, send_sem=ssem, recv_sem=rsem, device_id=partner, device_id_type=MESH
        ).wait_recv()

    loads = {}
    for i, (name, src, dst) in enumerate(
        (
            ("q", q_hbm, qz.at[0]),
            ("skv", skv_hbm, skv),
            ("pkv", pkv_hbm, kvb.at[0]),
            ("res", res_hbm, res),
            ("gain", gain_hbm, gain),
            ("ow", ow_hbm, ow),
            ("uw", uw_hbm, uw),
            ("dw", dw_hbm, dw),
        )
    ):
        loads[name] = pltpu.make_async_copy(src, dst, loc.at[i])
        loads[name].start()

    barrier = pltpu.get_barrier_semaphore()
    peers = [req_dev(d, 0) for d in Z_FAR] + [req_dev(0, d) for d in (1, 3)]
    peers += [chip_dev(o) for o in CHIPS] + [partner]
    for dev in peers:
        pl.semaphore_signal(barrier, inc=1, device_id=dev, device_id_type=MESH)
    pl.semaphore_wait(barrier, len(peers))

    right, left = req_dev(0, 1), req_dev(0, 3)
    for i, d in enumerate(Z_FAR):
        send(q_hbm, qz.at[4 - d], qzs.at[d - 1], qzr.at[3 - d], req_dev(d, 0))
    send(pkv_hbm.at[0], kvb.at[3, 0], kvs.at[0, 0], kvr.at[3, 0], right)
    send(pkv_hbm.at[1], kvb.at[1, 1], kvs.at[1, 0], kvr.at[1, 1], left)
    send(pkv_hbm.at[1], kvb.at[3, 1], kvs.at[0, 1], kvr.at[3, 1], right)
    send(pkv_hbm.at[0], kvb.at[1, 0], kvs.at[1, 1], kvr.at[1, 0], left)

    def arrive_kv(dx, part):
        arrive(kvb.at[dx, part], kvs.at[0, 0], kvr.at[dx, part])

    my_len = len_ref[me_r]
    slopes = [slope_of(2 * me_m + h) for h in range(2)]
    scale = float(DH) ** (-0.5)
    loads["q"].wait()
    loads["skv"].wait()
    key_i = lax.broadcasted_iota(jnp.int32, (S_MAX, ROWS), 0)
    slot_i = lax.broadcasted_iota(jnp.int32, (S_MAX, ROWS), 1)
    allowed = (key_i <= slot_i) & (key_i < my_len)
    gap = (slot_i - key_i).astype(F32)
    for h in range(2):
        cols = slice(h * DH, (h + 1) * DH)
        s = nt(skv[0, :, cols], qz[0, :, cols]) * scale - slopes[h] * gap
        s = jnp.where(allowed, s, NEG)
        m = jnp.max(s, axis=0, keepdims=True)
        w = jnp.where(allowed, jnp.exp(s - m), 0.0)
        sufs[2 * h : 2 * h + 1, :] = m
        sufs[2 * h + 1 : 2 * h + 2, :] = jnp.sum(w, axis=0, keepdims=True)
        sufo[h] = nn(skv[1, :, cols].T, w.astype(BF16))

    arrive_kv(3, 0)
    send(kvb.at[3, 0], kvb.at[2, 0], kvs.at[0, 2], kvr.at[2, 0], right)
    arrive_kv(1, 1)
    send(kvb.at[1, 1], kvb.at[2, 1], kvs.at[1, 2], kvr.at[2, 1], left)

    pkey = lax.broadcasted_iota(jnp.int32, (KB, ROWS), 0)
    pslot = lax.broadcasted_iota(jnp.int32, (KB, ROWS), 1)
    loads["pkv"].wait()
    for d in (1, 3, 2):
        arrive(qz.at[d], qzs.at[0], qzr.at[d - 1])

    def block_part(dx, dz):
        logical = own_ref[req_at(0, dx)]
        group = logical // PER_GROUP
        base = (logical - group * PER_GROUP) * KB
        valid = grp_ref[req_at(dz, 0)] == group
        dist = (P_SIZE - base + pslot - pkey).astype(F32)
        ms, ls, os = [], [], []
        for h in range(2):
            cols = slice(h * DH, (h + 1) * DH)
            s = nt(kvb[dx, 0, :, cols], qz[dz, :, cols]) * scale - slopes[h] * dist
            m = jnp.max(s, axis=0, keepdims=True)
            w = jnp.exp(s - m)
            ms.append(jnp.where(valid, m, NEG))
            ls.append(jnp.sum(w, axis=0, keepdims=True))
            os.append(nn(vt[h], w.astype(BF16)))
        return ms, ls, os

    def held(dz):
        at = 4 * dz
        return (
            [accs[at + 2 * h : at + 2 * h + 1, :] for h in range(2)],
            [accs[at + 2 * h + 1 : at + 2 * h + 2, :] for h in range(2)],
            [acco[dz, h] for h in range(2)],
        )

    def hold(dz, part):
        at = 4 * dz
        for h in range(2):
            accs[at + 2 * h : at + 2 * h + 1, :] = part[0][h]
            accs[at + 2 * h + 1 : at + 2 * h + 2, :] = part[1][h]
            acco[dz, h] = part[2][h]

    for dx in (0, 1, 3, 2):
        if dx == 1:
            arrive_kv(1, 0)
        if dx == 3:
            arrive_kv(3, 1)
        if dx == 2:
            arrive_kv(2, 0)
            arrive_kv(2, 1)
        for h in range(2):
            vt[h] = kvb[dx, 1, :, h * DH : (h + 1) * DH].T
        for dz in (2, 1, 3, 0):
            part = block_part(dx, dz)
            if dx != 0:
                part = combine([held(dz), part])
            if dx != 2 or dz == 0:
                hold(dz, part)
            else:
                ms, ls, os = part
                for h in range(2):
                    zsend[dz - 1, h * DH : (h + 1) * DH, :] = os[h].astype(BF16)
                zsend[dz - 1, COLS:SLOT, :] = pack_stats(ms, ls)
                send(zsend.at[dz - 1], zrecv.at[dz - 1], pzs.at[dz - 1], pzr.at[dz - 1], req_dev(dz, 0))

    suffix = ([sufs[0:1, :], sufs[2:3, :]], [sufs[1:2, :], sufs[3:4, :]], [sufo[0], sufo[1]])
    parts = [held(0), suffix]
    for dz in (1, 3, 2):
        arrive(zrecv.at[dz - 1], pzs.at[dz - 1], pzr.at[dz - 1])
        parts.append(read_slot(zrecv, (dz - 1,)))
    ms, ls, os = combine(parts)
    live = lax.broadcasted_iota(jnp.int32, (DH, ROWS), 1) < my_len
    for h in range(2):
        att_out[:, h * DH : (h + 1) * DH] = jnp.where(live, os[h] / ls[h], 0.0).T.astype(BF16)

    loads["res"].wait()
    loads["ow"].wait()
    respad[...] = jnp.zeros_like(respad)
    respad[:, pl.ds(pl.multiple_of(core * COLS, COLS), COLS)] = res[...].astype(F32)
    wide = 512

    def head_term(half, n):
        at = pl.multiple_of(half * HALF + n * wide, wide)
        t = nn(att_out[...], ow[:, pl.ds(at, wide)])
        return t + jnp.where(half * (HALF // wide) + n == chip, respad[...], 0.0)

    for n in range(HALF // wide):
        pre_s[n] = head_term(other, n).astype(BF16)
        send(pre_s.at[n], pre_r.at[n], p1s.at[n], p1r.at[n], partner)
    for n in range(HALF // wide):
        t = head_term(core, n)
        arrive(pre_r.at[n], p1s.at[n], p1r.at[n])
        rs_s[:, n * wide : (n + 1) * wide] = (t + pre_r[n].astype(F32)).astype(BF16)
    for i, off in enumerate(CHIPS):
        rows = pl.ds(pl.multiple_of(chip_at(off) * 16, 16), 16)
        send(rs_s.at[rows], rs_r.at[i], r1s.at[i], r1r.at[i], chip_dev(off))
    my_rows = pl.ds(pl.multiple_of(chip * 16, 16), 16)
    tot = rs_s[my_rows, :].astype(F32)
    for i in reversed(range(len(CHIPS))):
        arrive(rs_r.at[i], r1s.at[i], r1r.at[i])
        tot = tot + rs_r[i].astype(F32)

    mean_a = jnp.sum(tot, axis=1, keepdims=True) * (1.0 / HALF)
    cent = tot - mean_a
    m2_a = jnp.sum(cent * cent, axis=1, keepdims=True)
    lane = lax.broadcasted_iota(jnp.int32, (16, 128), 1)
    st_s[...] = jnp.where(lane < 64, mean_a, m2_a)
    send(st_s, st_r, sts.at[0], strv.at[0], partner)
    mixed[...] = tot
    loads["gain"].wait()
    arrive(st_r, sts.at[0], strv.at[0])
    mean_b, m2_b = st_r[:, 0:1], st_r[:, 64:65]
    diff = mean_a - mean_b
    mean = 0.5 * (mean_a + mean_b)
    var = (m2_a + m2_b + diff * diff * (HALF / 2)) * (1.0 / D)
    my_gain = gain[0:1, pl.ds(pl.multiple_of(core * HALF, HALF), HALF)]
    nall[core, my_rows, :] = ((tot - mean) * lax.rsqrt(var + 1e-05) * my_gain).astype(BF16)
    for i, off in enumerate(CHIPS):
        send(nall.at[core, my_rows], nall.at[core, my_rows], ags.at[i], agr.at[i], chip_dev(off))
    send(nall.at[core, my_rows], nall.at[core, my_rows], fws.at[7], fwr.at[7], partner)
    for i in reversed(range(len(CHIPS))):
        rows = pl.ds(pl.multiple_of(back(CHIPS[i]) * 16, 16), 16)
        arrive(nall.at[core, rows], ags.at[i], agr.at[i])
        send(nall.at[core, rows], nall.at[core, rows], fws.at[i], fwr.at[i], partner)

    loads["uw"].wait()
    acc = nn(nall[core], uw[pl.ds(pl.multiple_of(core * HALF, HALF), HALF), :])
    for i in range(len(CHIPS)):
        rows = pl.ds(pl.multiple_of(back(CHIPS[i]) * 16, 16), 16)
        arrive(nall.at[other, rows], fws.at[i], fwr.at[i])
    arrive(nall.at[other, my_rows], fws.at[7], fwr.at[7])
    acc = acc + nn(nall[other], uw[pl.ds(pl.multiple_of(other * HALF, HALF), HALF), :])
    hid = (acc * (0.5 * (1.0 + erf(acc * (0.5**0.5))))).astype(BF16)

    loads["dw"].wait()
    order = CHIPS + ((0, 0),)

    def unit_term(off, which):
        block = chip_at(off) * 2 + which
        t = nn(hid, dw[:, pl.ds(pl.multiple_of(block * COLS, COLS), COLS)])
        inner = lax.rem(block, NCHIP)
        add = mixed[:, pl.ds(pl.multiple_of(inner * COLS, COLS), COLS)]
        tmp[...] = t
        tmp[my_rows, :] = tmp[my_rows, :] + jnp.where(block // NCHIP == core, add, 0.0)
        return tmp[...]

    for i, off in enumerate(order):
        pre2_s[i] = unit_term(off, other).astype(BF16)
        send(pre2_s.at[i], pre2_r.at[i], p2s.at[i], p2r.at[i], partner)
    out = None
    for i, off in enumerate(order):
        t = unit_term(off, core)
        arrive(pre2_r.at[i], p2s.at[i], p2r.at[i])
        t = t + pre2_r[i].astype(F32)
        if i < len(CHIPS):
            rs2_s[i] = t.astype(BF16)
            send(rs2_s.at[i], rs2_r.at[i], r2s.at[i], r2r.at[i], chip_dev(off))
        else:
            out = t
    for i in reversed(range(len(CHIPS))):
        arrive(rs2_r.at[i], r2s.at[i], r2r.at[i])
        out = out + rs2_r[i].astype(F32)
    row_live = lax.broadcasted_iota(jnp.int32, (ROWS, COLS), 0) < my_len
    lay_out[...] = jnp.where(row_live, out, 0.0).astype(BF16)
    for cp in sends:
        cp.wait_send()


def shards(
    queries,
    suffix_kv,
    prefix_kv,
    resid,
    ln_gain,
    out_weight,
    up_weight,
    down_weight,
    lengths,
    req_group,
    prefix_owner,
):
    smem = pl.BlockSpec(memory_space=pltpu.SMEM)
    anym = pl.BlockSpec(memory_space=pl.ANY)
    vmem = pl.BlockSpec(memory_space=pltpu.VMEM)
    dma = pltpu.SemaphoreType.DMA
    vm = pltpu.VMEM
    n = HALF // 512
    nc = len(CHIPS)
    return pl.pallas_call(
        kernel,
        out_shape=[jax.ShapeDtypeStruct((ROWS, COLS), BF16)] * 2,
        in_specs=[smem] * 3 + [anym] * 8,
        out_specs=[vmem] * 2,
        scratch_shapes=[
            vm((NZH, ROWS, COLS), BF16),
            vm((2, S_MAX, COLS), BF16),
            vm((NX, 2, KB, COLS), BF16),
            vm((ROWS, COLS), BF16),
            vm((1, D), F32),
            vm((COLS, D), BF16),
            vm((D, UNITS), BF16),
            vm((UNITS, D), BF16),
            vm((2, DH, KB), BF16),
            vm((2, DH, ROWS), F32),
            vm((8, ROWS), F32),
            vm((NZH, 2, DH, ROWS), F32),
            vm((16, ROWS), F32),
            vm((3, SLOT, ROWS), BF16),
            vm((3, SLOT, ROWS), BF16),
            vm((ROWS, 512), F32),
            vm((n, ROWS, 512), BF16),
            vm((n, ROWS, 512), BF16),
            vm((ROWS, HALF), BF16),
            vm((nc, 16, HALF), BF16),
            vm((16, 128), F32),
            vm((16, 128), F32),
            vm((16, HALF), F32),
            vm((2, ROWS, HALF), BF16),
            vm((ROWS, COLS), F32),
            vm((8, ROWS, COLS), BF16),
            vm((8, ROWS, COLS), BF16),
            vm((nc, ROWS, COLS), BF16),
            vm((nc, ROWS, COLS), BF16),
            dma((8,)),
            dma((3,)),
            dma((3,)),
            dma((2, 3)),
            dma((NX, 2)),
            dma((3,)),
            dma((3,)),
            dma((n,)),
            dma((n,)),
            dma((nc,)),
            dma((nc,)),
            dma((1,)),
            dma((1,)),
            dma((nc,)),
            dma((nc,)),
            dma((8,)),
            dma((8,)),
            dma((8,)),
            dma((8,)),
            dma((nc,)),
            dma((nc,)),
        ],
        compiler_params=pltpu.CompilerParams(
            collective_id=0, has_side_effects=True, vmem_limit_bytes=56 * 2**20
        ),
        name="prefill_layer",
    )(
        lengths,
        req_group,
        prefix_owner,
        queries,
        suffix_kv,
        prefix_kv,
        resid,
        ln_gain.reshape(1, D),
        out_weight,
        up_weight,
        down_weight,
    )


def solution(mesh):
    placed = (
        P("req", "mp"),
        P(None, "req", "mp"),
        P(None, "req", "mp"),
        P("req", "mp"),
        P(),
        P("mp", None),
        P(None, "mp"),
        P("mp", None),
        P(),
        P(),
        P(),
    )
    return jax.shard_map(
        shards,
        mesh=mesh,
        in_specs=placed,
        out_specs=(P("req", "mp"), P("req", "mp")),
        check_vma=False,
    )
```

```python
import functools

import jax
import jax.numpy as jnp
from jax import lax
from jax.experimental import pallas as pl
from jax.experimental.pallas import tpu as pltpu
from jax.sharding import PartitionSpec as P

MESH = pl.DeviceIdType.MESH
H = 32
DH = 128
KB = 512
S_MAX = 128
P_SIZE = 2048
PER_GROUP = P_SIZE // KB
NX = 4
NZH = 4
NY = 4
NZL = 2
NCHIP = NY * NZL
NREQ = NX * NZH
NEG = -1e30
ROWS = S_MAX
COLS = 2 * DH
D = 4096
HALF = D // 2
UNITS = 512
HR = ROWS // 2
STAT = 16
SLOT = COLS + STAT

Z_FAR = (2, 1, 3)
CHIPS = ((1, 2), (1, 1), (1, 3), (0, 2), (1, 0), (0, 1), (0, 3))

F32 = jnp.float32
BF16 = jnp.bfloat16


def nt(a, b):
    return lax.dot_general(a, b, (((1,), (1,)), ((), ())), preferred_element_type=F32)


def nn(a, b):
    return lax.dot_general(a, b, (((1,), (0,)), ((), ())), preferred_element_type=F32)


def slope_of(head):
    k = head + 1
    whole, part = k // 4, lax.rem(k, 4)
    out = jnp.float32(1.0)
    for i in range(1, 9):
        out = jnp.where(whole == i, jnp.float32(2.0**-i), out)
    frac = jnp.float32(1.0)
    for i in range(1, 4):
        frac = jnp.where(part == i, jnp.float32(2.0 ** (-0.25 * i)), frac)
    return out * frac


def split3(v):
    hi = v.astype(BF16).astype(F32)
    rest = v - hi
    mid = rest.astype(BF16).astype(F32)
    return hi, mid, rest - mid


def pack_stats(ms, ls):
    row = lax.broadcasted_iota(jnp.int32, (STAT, ROWS), 0)
    out = jnp.zeros((STAT, ROWS), F32)
    at = 0
    for m, l in zip(ms, ls):
        for part in split3(m) + split3(l):
            out = jnp.where(row == at, part, out)
            at += 1
    return out.astype(BF16)


def unpack_stats(block):
    st = block.astype(F32)
    ms, ls = [], []
    for h in range(2):
        at = 6 * h
        ms.append(st[at : at + 1] + st[at + 1 : at + 2] + st[at + 2 : at + 3])
        ls.append(st[at + 3 : at + 4] + st[at + 4 : at + 5] + st[at + 5 : at + 6])
    return ms, ls


def combine(parts):
    ms, ls, os = [], [], []
    for h in range(2):
        m = parts[0][0][h]
        for part in parts[1:]:
            m = jnp.maximum(m, part[0][h])
        l, o = None, None
        for part in parts:
            scale = jnp.exp(part[0][h] - m)
            pl_, po = part[1][h] * scale, part[2][h] * scale
            l = pl_ if l is None else l + pl_
            o = po if o is None else o + po
        ms.append(m)
        ls.append(l)
        os.append(o)
    return ms, ls, os


def read_slot(ref, lead):
    ms, ls = unpack_stats(ref[lead + (pl.ds(COLS, STAT), slice(None))])
    os = [ref[lead + (pl.ds(h * DH, DH), slice(None))].astype(F32) for h in range(2)]
    return ms, ls, os


def erf(x):
    return lax.erf(x)


def kernel(
    len_ref,
    grp_ref,
    own_ref,
    q_hbm,
    skv_hbm,
    pkv_hbm,
    res_hbm,
    gain_hbm,
    ow_hbm,
    uw_hbm,
    dw_hbm,
    att_out,
    lay_out,
    qz,
    skv,
    kvb,
    res,
    gain,
    ow,
    uw,
    dw,
    vt,
    sufo,
    sufs,
    acco,
    accs,
    zsend,
    zrecv,
    respad,
    pre_s,
    pre_r,
    rs_s,
    rs_r,
    st_s,
    st_r,
    mixed,
    nall,
    tmp,
    outk,
    pre2_s,
    pre2_r,
    rs2_s,
    rs2_r,
    loc,
    qzs,
    qzr,
    kvs,
    kvr,
    pzs,
    pzr,
    p1s,
    p1r,
    r1s,
    r1r,
    sts,
    strv,
    ags,
    agr,
    fws,
    fwr,
    p2s,
    p2r,
    r2s,
    r2r,
):
    me_r = lax.axis_index("req")
    me_m = lax.axis_index("mp")
    zh, x = me_r // NX, lax.rem(me_r, NX)
    core = lax.rem(me_m, 2)
    chip = me_m // 2
    zl, y = chip // NY, lax.rem(chip, NY)
    other = 1 - core

    def req_at(dz, dx):
        return lax.rem(zh + dz, NZH) * NX + lax.rem(x + dx, NX)

    def req_dev(dz, dx):
        return (req_at(dz, dx), me_m)

    def chip_at(off):
        return lax.rem(zl + off[0], NZL) * NY + lax.rem(y + off[1], NY)

    def back(off):
        return lax.rem(zl + off[0], NZL) * NY + lax.rem(y + NY - off[1], NY)

    def chip_dev(off):
        return (me_r, chip_at(off) * 2 + core)

    partner = (me_r, chip * 2 + other)
    sends = []

    def send(src, dst, ssem, rsem, dev):
        cp = pltpu.make_async_remote_copy(
            src_ref=src, dst_ref=dst, send_sem=ssem, recv_sem=rsem, device_id=dev, device_id_type=MESH
        )
        cp.start()
        sends.append(cp)

    def arrive(dst, ssem, rsem):
        pltpu.make_async_remote_copy(
            src_ref=dst, dst_ref=dst, send_sem=ssem, recv_sem=rsem, device_id=partner, device_id_type=MESH
        ).wait_recv()

    loads = {}
    for i, (name, src, dst) in enumerate(
        (
            ("q", q_hbm, qz.at[0]),
            ("skv", skv_hbm, skv),
            ("pkv", pkv_hbm, kvb.at[0]),
            ("res", res_hbm, res),
            ("gain", gain_hbm, gain),
            ("ow", ow_hbm, ow),
            ("uw", uw_hbm, uw),
            ("dw", dw_hbm, dw),
        )
    ):
        loads[name] = pltpu.make_async_copy(src, dst, loc.at[i])
        loads[name].start()

    barrier = pltpu.get_barrier_semaphore()
    peers = [req_dev(d, 0) for d in Z_FAR] + [req_dev(0, d) for d in (1, 3)]
    peers += [chip_dev(o) for o in CHIPS] + [partner]
    for dev in peers:
        pl.semaphore_signal(barrier, inc=1, device_id=dev, device_id_type=MESH)
    pl.semaphore_wait(barrier, len(peers))

    right, left = req_dev(0, 1), req_dev(0, 3)
    for i, d in enumerate(Z_FAR):
        send(q_hbm, qz.at[4 - d], qzs.at[d - 1], qzr.at[3 - d], req_dev(d, 0))
    send(pkv_hbm.at[0], kvb.at[3, 0], kvs.at[0, 0], kvr.at[3, 0], right)
    send(pkv_hbm.at[1], kvb.at[1, 1], kvs.at[1, 0], kvr.at[1, 1], left)
    send(pkv_hbm.at[1], kvb.at[3, 1], kvs.at[0, 1], kvr.at[3, 1], right)
    send(pkv_hbm.at[0], kvb.at[1, 0], kvs.at[1, 1], kvr.at[1, 0], left)

    def arrive_kv(dx, part):
        arrive(kvb.at[dx, part], kvs.at[0, 0], kvr.at[dx, part])

    my_len = len_ref[me_r]
    slopes = [slope_of(2 * me_m + h) for h in range(2)]
    scale = float(DH) ** (-0.5)
    loads["q"].wait()
    loads["skv"].wait()
    key_i = lax.broadcasted_iota(jnp.int32, (S_MAX, ROWS), 0)
    slot_i = lax.broadcasted_iota(jnp.int32, (S_MAX, ROWS), 1)
    allowed = (key_i <= slot_i) & (key_i < my_len)
    gap = (slot_i - key_i).astype(F32)
    for h in range(2):
        cols = slice(h * DH, (h + 1) * DH)
        s = nt(skv[0, :, cols], qz[0, :, cols]) * scale - slopes[h] * gap
        s = jnp.where(allowed, s, NEG)
        m = jnp.max(s, axis=0, keepdims=True)
        w = jnp.where(allowed, jnp.exp(s - m), 0.0)
        sufs[2 * h : 2 * h + 1, :] = m
        sufs[2 * h + 1 : 2 * h + 2, :] = jnp.sum(w, axis=0, keepdims=True)
        sufo[h] = nn(skv[1, :, cols].T, w.astype(BF16))

    arrive_kv(3, 0)
    send(kvb.at[3, 0], kvb.at[2, 0], kvs.at[0, 2], kvr.at[2, 0], right)
    arrive_kv(1, 1)
    send(kvb.at[1, 1], kvb.at[2, 1], kvs.at[1, 2], kvr.at[2, 1], left)

    pkey = lax.broadcasted_iota(jnp.int32, (KB, ROWS), 0)
    pslot = lax.broadcasted_iota(jnp.int32, (KB, ROWS), 1)
    loads["pkv"].wait()
    for d in (1, 3, 2):
        arrive(qz.at[d], qzs.at[0], qzr.at[d - 1])

    def block_part(dx, dz):
        logical = own_ref[req_at(0, dx)]
        group = logical // PER_GROUP
        base = (logical - group * PER_GROUP) * KB
        valid = grp_ref[req_at(dz, 0)] == group
        dist = (P_SIZE - base + pslot - pkey).astype(F32)
        ms, ls, os = [], [], []
        for h in range(2):
            cols = slice(h * DH, (h + 1) * DH)
            s = nt(kvb[dx, 0, :, cols], qz[dz, :, cols]) * scale - slopes[h] * dist
            m = jnp.max(s, axis=0, keepdims=True)
            w = jnp.exp(s - m)
            ms.append(jnp.where(valid, m, NEG))
            ls.append(jnp.sum(w, axis=0, keepdims=True))
            os.append(nn(vt[h], w.astype(BF16)))
        return ms, ls, os

    def held(dz):
        at = 4 * dz
        return (
            [accs[at + 2 * h : at + 2 * h + 1, :] for h in range(2)],
            [accs[at + 2 * h + 1 : at + 2 * h + 2, :] for h in range(2)],
            [acco[dz, h] for h in range(2)],
        )

    def hold(dz, part):
        at = 4 * dz
        for h in range(2):
            accs[at + 2 * h : at + 2 * h + 1, :] = part[0][h]
            accs[at + 2 * h + 1 : at + 2 * h + 2, :] = part[1][h]
            acco[dz, h] = part[2][h]

    for dx in (0, 1, 3, 2):
        if dx == 1:
            arrive_kv(1, 0)
        if dx == 3:
            arrive_kv(3, 1)
        if dx == 2:
            arrive_kv(2, 0)
            arrive_kv(2, 1)
        for h in range(2):
            vt[h] = kvb[dx, 1, :, h * DH : (h + 1) * DH].T
        for dz in (2, 1, 3, 0):
            part = block_part(dx, dz)
            if dx != 0:
                part = combine([held(dz), part])
            if dx != 2 or dz == 0:
                hold(dz, part)
            else:
                ms, ls, os = part
                for h in range(2):
                    zsend[dz - 1, h * DH : (h + 1) * DH, :] = os[h].astype(BF16)
                zsend[dz - 1, COLS:SLOT, :] = pack_stats(ms, ls)
                send(zsend.at[dz - 1], zrecv.at[dz - 1], pzs.at[dz - 1], pzr.at[dz - 1], req_dev(dz, 0))

    suffix = ([sufs[0:1, :], sufs[2:3, :]], [sufs[1:2, :], sufs[3:4, :]], [sufo[0], sufo[1]])
    parts = [held(0), suffix]
    for dz in (1, 3, 2):
        arrive(zrecv.at[dz - 1], pzs.at[dz - 1], pzr.at[dz - 1])
        parts.append(read_slot(zrecv, (dz - 1,)))
    ms, ls, os = combine(parts)
    live = lax.broadcasted_iota(jnp.int32, (DH, ROWS), 1) < my_len
    for h in range(2):
        att_out[:, h * DH : (h + 1) * DH] = jnp.where(live, os[h] / ls[h], 0.0).T.astype(BF16)

    loads["res"].wait()
    loads["ow"].wait()
    respad[...] = jnp.zeros_like(respad)
    respad[:, pl.ds(pl.multiple_of(core * COLS, COLS), COLS)] = res[...].astype(F32)
    wide = 512

    def head_term(half, n, rows):
        at = pl.multiple_of(half * HALF + n * wide, wide)
        t = nn(att_out[rows, :], ow[:, pl.ds(at, wide)])
        return t + jnp.where(half * (HALF // wide) + n == chip, respad[rows, :], 0.0)

    def rows_of(a):
        return slice(a * HR, (a + 1) * HR)

    for n in (0, 2, 1, 3):
        pre_s[n] = head_term(other, n, slice(None)).astype(BF16)
        send(pre_s.at[n], pre_r.at[n], p1s.at[n], p1r.at[n], partner)

    for a in range(2):
        for n in range(2):
            terms = []
            for cn in (n, n + 2):
                t = head_term(core, cn, rows_of(a))
                if a == 0:
                    arrive(pre_r.at[cn], p1s.at[cn], p1r.at[cn])
                terms.append(t + pre_r[cn, rows_of(a), :].astype(F32))
            for k in range(NCHIP):
                rs_s[a, k, :, n * wide : (n + 1) * wide] = jnp.concatenate(
                    [t[8 * k : 8 * k + 8] for t in terms], axis=0
                ).astype(BF16)
        for i, off in enumerate(CHIPS):
            send(rs_s.at[a, chip_at(off)], rs_r.at[a, i], r1s.at[a, i], r1r.at[a, i], chip_dev(off))
    loads["gain"].wait()
    gain_at = pl.multiple_of(core * HALF, HALF)
    gain_16 = jnp.concatenate(
        [
            jnp.broadcast_to(gain[0:1, pl.ds(gain_at, HALF // 2)], (8, HALF // 2)),
            jnp.broadcast_to(gain[0:1, pl.ds(gain_at + HALF // 2, HALF // 2)], (8, HALF // 2)),
        ],
        axis=0,
    )

    def both(v):
        return v[0:8] + v[8:16]

    def twice(v):
        return jnp.concatenate([v, v], axis=0)

    lane = lax.broadcasted_iota(jnp.int32, (8, 128), 1)
    for a in range(2):
        tot = rs_s[a, chip].astype(F32)
        for i in reversed(range(len(CHIPS))):
            arrive(rs_r.at[a, i], r1s.at[a, i], r1r.at[a, i])
            tot = tot + rs_r[a, i].astype(F32)
        mean_a = both(jnp.sum(tot, axis=1, keepdims=True)) * (1.0 / HALF)
        cent = tot - twice(mean_a)
        m2_a = both(jnp.sum(cent * cent, axis=1, keepdims=True))
        st_s[a] = jnp.where(lane < 64, mean_a, m2_a)
        send(st_s.at[a], st_r.at[a], sts.at[a], strv.at[a], partner)
        mixed[a, :, 0 : HALF // 2] = tot[0:8]
        mixed[a, :, HALF // 2 : HALF] = tot[8:16]
        arrive(st_r.at[a], sts.at[a], strv.at[a])
        mean_b, m2_b = st_r[a, :, 0:1], st_r[a, :, 64:65]
        diff = mean_a - mean_b
        mean = 0.5 * (mean_a + mean_b)
        var = (m2_a + m2_b + diff * diff * (HALF / 2)) * (1.0 / D)
        nall[a, core, chip] = ((tot - twice(mean)) * twice(lax.rsqrt(var + 1e-05)) * gain_16).astype(BF16)
        mine = nall.at[a, core, chip]
        for i, off in enumerate(CHIPS):
            send(mine, mine, ags.at[a, i], agr.at[a, i], chip_dev(off))
        send(mine, mine, fws.at[a, 7], fwr.at[a, 7], partner)

    def up_half(a, half):
        blocks = [nall[a, half, k].astype(F32) for k in range(NCHIP)]
        out = None
        for part in range(2):
            lhs = jnp.concatenate([v[8 * part : 8 * part + 8] for v in blocks], axis=0).astype(BF16)
            at = pl.multiple_of(half * HALF + part * (HALF // 2), HALF // 2)
            t = nn(lhs, uw[pl.ds(at, HALF // 2), :])
            out = t if out is None else out + t
        return out

    order = CHIPS + ((0, 0),)

    def unit_term(hid, a, off, which):
        block = chip_at(off) * 2 + which
        tmp[...] = nn(hid, dw[:, pl.ds(pl.multiple_of(block * COLS, COLS), COLS)])
        inner = lax.rem(block, NCHIP)
        add = mixed[a, :, pl.ds(pl.multiple_of(inner * COLS, COLS), COLS)]
        mine = pl.ds(pl.multiple_of(chip * 8, 8), 8)
        tmp[mine, :] = tmp[mine, :] + jnp.where(block // NCHIP == core, add, 0.0)
        return tmp[...]

    for a in range(2):
        for i in reversed(range(len(CHIPS))):
            src = nall.at[a, core, back(CHIPS[i])]
            arrive(src, ags.at[a, i], agr.at[a, i])
            send(src, src, fws.at[a, i], fwr.at[a, i], partner)
        if a == 0:
            loads["uw"].wait()
        acc = up_half(a, core)
        for i in range(len(CHIPS)):
            arrive(nall.at[a, other, back(CHIPS[i])], fws.at[a, i], fwr.at[a, i])
        arrive(nall.at[a, other, chip], fws.at[a, 7], fwr.at[a, 7])
        acc = acc + up_half(a, other)
        hid = (acc * (0.5 * (1.0 + erf(acc * (0.5**0.5))))).astype(BF16)
        if a == 0:
            loads["dw"].wait()
        for i, off in enumerate(order):
            pre2_s[a, i] = unit_term(hid, a, off, other).astype(BF16)
            send(pre2_s.at[a, i], pre2_r.at[a, i], p2s.at[a, i], p2r.at[a, i], partner)
        for i, off in enumerate(order):
            t = unit_term(hid, a, off, core)
            arrive(pre2_r.at[a, i], p2s.at[a, i], p2r.at[a, i])
            t = t + pre2_r[a, i].astype(F32)
            if i < len(CHIPS):
                rs2_s[a, i] = t.astype(BF16)
                send(rs2_s.at[a, i], rs2_r.at[a, i], r2s.at[a, i], r2r.at[a, i], chip_dev(off))
            else:
                outk[a] = t
    row_i = lax.broadcasted_iota(jnp.int32, (HR, COLS), 0)
    for a in range(2):
        out = outk[a]
        for i in reversed(range(len(CHIPS))):
            arrive(rs2_r.at[a, i], r2s.at[a, i], r2r.at[a, i])
            out = out + rs2_r[a, i].astype(F32)
        lay_out[rows_of(a), :] = jnp.where(row_i + a * HR < my_len, out, 0.0).astype(BF16)
    for cp in sends:
        cp.wait_send()


def shards(
    queries,
    suffix_kv,
    prefix_kv,
    resid,
    ln_gain,
    out_weight,
    up_weight,
    down_weight,
    lengths,
    req_group,
    prefix_owner,
):
    smem = pl.BlockSpec(memory_space=pltpu.SMEM)
    anym = pl.BlockSpec(memory_space=pl.ANY)
    vmem = pl.BlockSpec(memory_space=pltpu.VMEM)
    dma = pltpu.SemaphoreType.DMA
    vm = pltpu.VMEM
    n = HALF // 512
    nc = len(CHIPS)
    return pl.pallas_call(
        kernel,
        out_shape=[jax.ShapeDtypeStruct((ROWS, COLS), BF16)] * 2,
        in_specs=[smem] * 3 + [anym] * 8,
        out_specs=[vmem] * 2,
        scratch_shapes=[
            vm((NZH, ROWS, COLS), BF16),
            vm((2, S_MAX, COLS), BF16),
            vm((NX, 2, KB, COLS), BF16),
            vm((ROWS, COLS), BF16),
            vm((1, D), F32),
            vm((COLS, D), BF16),
            vm((D, UNITS), BF16),
            vm((UNITS, D), BF16),
            vm((2, DH, KB), BF16),
            vm((2, DH, ROWS), F32),
            vm((8, ROWS), F32),
            vm((NZH, 2, DH, ROWS), F32),
            vm((16, ROWS), F32),
            vm((3, SLOT, ROWS), BF16),
            vm((3, SLOT, ROWS), BF16),
            vm((ROWS, 512), F32),
            vm((n, ROWS, 512), BF16),
            vm((n, ROWS, 512), BF16),
            vm((2, NCHIP, 16, HALF // 2), BF16),
            vm((2, nc, 16, HALF // 2), BF16),
            vm((2, 8, 128), F32),
            vm((2, 8, 128), F32),
            vm((2, 8, HALF), F32),
            vm((2, 2, NCHIP, 16, HALF // 2), BF16),
            vm((HR, COLS), F32),
            vm((2, HR, COLS), F32),
            vm((2, 8, HR, COLS), BF16),
            vm((2, 8, HR, COLS), BF16),
            vm((2, nc, HR, COLS), BF16),
            vm((2, nc, HR, COLS), BF16),
            dma((8,)),
            dma((3,)),
            dma((3,)),
            dma((2, 3)),
            dma((NX, 2)),
            dma((3,)),
            dma((3,)),
            dma((n,)),
            dma((n,)),
            dma((2, nc)),
            dma((2, nc)),
            dma((2,)),
            dma((2,)),
            dma((2, nc)),
            dma((2, nc)),
            dma((2, 8)),
            dma((2, 8)),
            dma((2, 8)),
            dma((2, 8)),
            dma((2, nc)),
            dma((2, nc)),
        ],
        compiler_params=pltpu.CompilerParams(
            collective_id=0, has_side_effects=True, vmem_limit_bytes=56 * 2**20
        ),
        name="prefill_layer",
    )(
        lengths,
        req_group,
        prefix_owner,
        queries,
        suffix_kv,
        prefix_kv,
        resid,
        ln_gain.reshape(1, D),
        out_weight,
        up_weight,
        down_weight,
    )


def solution(mesh):
    placed = (
        P("req", "mp"),
        P(None, "req", "mp"),
        P(None, "req", "mp"),
        P("req", "mp"),
        P(),
        P("mp", None),
        P(None, "mp"),
        P("mp", None),
        P(),
        P(),
        P(),
    )
    return jax.shard_map(
        shards,
        mesh=mesh,
        in_specs=placed,
        out_specs=(P("req", "mp"), P("req", "mp")),
        check_vma=False,
    )
```

```python
import functools

import jax
import jax.numpy as jnp
from jax import lax
from jax.experimental import pallas as pl
from jax.experimental.pallas import tpu as pltpu
from jax.sharding import PartitionSpec as P

MESH = pl.DeviceIdType.MESH
H = 32
DH = 128
KB = 512
S_MAX = 128
P_SIZE = 2048
PER_GROUP = P_SIZE // KB
NX = 4
NZH = 4
NY = 4
NZL = 2
NCHIP = NY * NZL
NREQ = NX * NZH
NEG = -1e30
ROWS = S_MAX
COLS = 2 * DH
D = 4096
HALF = D // 2
UNITS = 512
HR = ROWS // 2
STAT = 16
SLOT = DH + STAT
LOG2E = 1.4426950408889634

Z_FAR = (2, 1, 3)
CHIPS = ((1, 2), (1, 1), (1, 3), (0, 2), (1, 0), (0, 1), (0, 3))

F32 = jnp.float32
BF16 = jnp.bfloat16


def nt(a, b):
    return lax.dot_general(a, b, (((1,), (1,)), ((), ())), preferred_element_type=F32)


def nn(a, b):
    return lax.dot_general(a, b, (((1,), (0,)), ((), ())), preferred_element_type=F32)


def head(h):
    return slice(h * DH, (h + 1) * DH)


def slope_of(index):
    k = index + 1
    whole, part = k // 4, lax.rem(k, 4)
    out = jnp.float32(1.0)
    for i in range(1, 9):
        out = jnp.where(whole == i, jnp.float32(2.0**-i), out)
    frac = jnp.float32(1.0)
    for i in range(1, 4):
        frac = jnp.where(part == i, jnp.float32(2.0 ** (-0.25 * i)), frac)
    return out * frac


def split3(v):
    hi = v.astype(BF16).astype(F32)
    rest = v - hi
    mid = rest.astype(BF16).astype(F32)
    return hi, mid, rest - mid


def pack_stats(m, l):
    row = lax.broadcasted_iota(jnp.int32, (STAT, ROWS), 0)
    out = jnp.zeros((STAT, ROWS), F32)
    for at, part in enumerate(split3(m) + split3(l)):
        out = jnp.where(row == at, part, out)
    return out.astype(BF16)


def combine(parts):
    m = parts[0][0]
    for part in parts[1:]:
        m = jnp.maximum(m, part[0])
    l, o = None, None
    for part in parts:
        scale = jnp.exp2(part[0] - m)
        l = part[1] * scale if l is None else l + part[1] * scale
        o = part[2] * scale if o is None else o + part[2] * scale
    return m, l, o


def read_slot(ref, lead):
    st = ref[lead + (pl.ds(DH, STAT), slice(None))].astype(F32)
    m = st[0:1] + st[1:2] + st[2:3]
    l = st[3:4] + st[4:5] + st[5:6]
    return m, l, ref[lead + (pl.ds(0, DH), slice(None))].astype(F32)


def erf(x):
    return lax.erf(x)


def kernel(
    len_ref,
    grp_ref,
    own_ref,
    q_hbm,
    skv_hbm,
    pkv_hbm,
    res_hbm,
    gain_hbm,
    ow_hbm,
    uw_hbm,
    dw_hbm,
    att_out,
    lay_out,
    qz,
    skv,
    kvb,
    res,
    gain,
    ow,
    uw,
    dw,
    vt,
    sufo,
    sufs,
    kbias,
    sbuf,
    acco,
    accs,
    zsend,
    zrecv,
    respad,
    pre_s,
    pre_r,
    rs_s,
    rs_r,
    st_s,
    st_r,
    mixed,
    nall,
    tmp,
    outk,
    pre2_s,
    pre2_r,
    rs2_s,
    rs2_r,
    loc,
    qzs,
    qzr,
    kvs,
    fks,
    kvr,
    pzs,
    pzr,
    p1s,
    p1r,
    r1s,
    r1r,
    sts,
    strv,
    ags,
    agr,
    fws,
    fwr,
    p2s,
    p2r,
    r2s,
    r2r,
):
    me_r = lax.axis_index("req")
    me_m = lax.axis_index("mp")
    zh, x = me_r // NX, lax.rem(me_r, NX)
    core = lax.rem(me_m, 2)
    chip = me_m // 2
    zl, y = chip // NY, lax.rem(chip, NY)
    other = 1 - core

    def req_at(dz, dx):
        return lax.rem(zh + dz, NZH) * NX + lax.rem(x + dx, NX)

    def req_dev(dz, dx):
        return (req_at(dz, dx), me_m)

    def chip_at(off):
        return lax.rem(zl + off[0], NZL) * NY + lax.rem(y + off[1], NY)

    def back(off):
        return lax.rem(zl + off[0], NZL) * NY + lax.rem(y + NY - off[1], NY)

    def chip_dev(off):
        return (me_r, chip_at(off) * 2 + core)

    partner = (me_r, chip * 2 + other)
    sends = []

    def send(src, dst, ssem, rsem, dev):
        cp = pltpu.make_async_remote_copy(
            src_ref=src, dst_ref=dst, send_sem=ssem, recv_sem=rsem, device_id=dev, device_id_type=MESH
        )
        cp.start()
        sends.append(cp)

    def arrive(dst, ssem, rsem):
        pltpu.make_async_remote_copy(
            src_ref=dst, dst_ref=dst, send_sem=ssem, recv_sem=rsem, device_id=partner, device_id_type=MESH
        ).wait_recv()

    loads = {}
    for i, (name, src, dst) in enumerate(
        (
            ("q", q_hbm, qz.at[0]),
            ("skv", skv_hbm, skv),
            ("pkv00", pkv_hbm.at[0, :, head(0)], kvb.at[0, 0, 0]),
            ("pkv10", pkv_hbm.at[1, :, head(0)], kvb.at[0, 1, 0]),
            ("pkv01", pkv_hbm.at[0, :, head(1)], kvb.at[0, 0, 1]),
            ("pkv11", pkv_hbm.at[1, :, head(1)], kvb.at[0, 1, 1]),
            ("res", res_hbm, res),
            ("gain", gain_hbm, gain),
            ("ow", ow_hbm, ow),
            ("uw", uw_hbm, uw),
            ("dw", dw_hbm, dw),
        )
    ):
        loads[name] = pltpu.make_async_copy(src, dst, loc.at[i])
        loads[name].start()

    barrier = pltpu.get_barrier_semaphore()
    peers = [req_dev(d, 0) for d in Z_FAR] + [req_dev(0, d) for d in (1, 3)]
    peers += [chip_dev(o) for o in CHIPS] + [partner]
    for dev in peers:
        pl.semaphore_signal(barrier, inc=1, device_id=dev, device_id_type=MESH)
    pl.semaphore_wait(barrier, len(peers))

    right, left = req_dev(0, 1), req_dev(0, 3)
    for i, d in enumerate(Z_FAR):
        send(q_hbm, qz.at[4 - d], qzs.at[d - 1], qzr.at[3 - d], req_dev(d, 0))
    for h in range(2):
        for first in range(2):
            k, v = first, 1 - first
            send(pkv_hbm.at[k, :, head(h)], kvb.at[3, k, h], kvs.at[0, k, h], kvr.at[3, k, h], right)
            send(pkv_hbm.at[v, :, head(h)], kvb.at[1, v, h], kvs.at[1, v, h], kvr.at[1, v, h], left)

    def arrive_kv(dx, part, h):
        arrive(kvb.at[dx, part, h], kvs.at[0, 0, 0], kvr.at[dx, part, h])

    my_len = len_ref[me_r]
    slopes = [slope_of(2 * me_m + h) for h in range(2)]
    scale = float(DH) ** (-0.5)
    loads["q"].wait()
    loads["skv"].wait()
    key_i = lax.broadcasted_iota(jnp.int32, (S_MAX, ROWS), 0)
    slot_i = lax.broadcasted_iota(jnp.int32, (S_MAX, ROWS), 1)
    allowed = (key_i <= slot_i) & (key_i < my_len)
    gap = (slot_i - key_i).astype(F32)
    pkey = lax.broadcasted_iota(jnp.int32, (KB, ROWS), 0).astype(F32)
    for h in range(2):
        s = (nt(skv[0, :, head(h)], qz[0, :, head(h)]) * scale - slopes[h] * gap) * LOG2E
        s = jnp.where(allowed, s, NEG)
        m = jnp.max(s, axis=0, keepdims=True)
        w = jnp.where(allowed, jnp.exp2(s - m), 0.0)
        sufs[2 * h : 2 * h + 1, :] = m
        sufs[2 * h + 1 : 2 * h + 2, :] = jnp.sum(w, axis=0, keepdims=True)
        sufo[h] = nn(skv[1, :, head(h)].T, w.astype(BF16))
        kbias[h] = pkey * (slopes[h] * LOG2E)

    for h in range(2):
        arrive_kv(3, 0, h)
        send(kvb.at[3, 0, h], kvb.at[2, 0, h], fks.at[0, h], kvr.at[2, 0, h], right)
        arrive_kv(1, 1, h)
        send(kvb.at[1, 1, h], kvb.at[2, 1, h], fks.at[1, h], kvr.at[2, 1, h], left)

    pslot = lax.broadcasted_iota(jnp.int32, (1, ROWS), 1)
    for name in ("pkv00", "pkv01", "pkv10", "pkv11"):
        loads[name].wait()
    for d in (1, 3, 2):
        arrive(qz.at[d], qzs.at[0], qzr.at[d - 1])
    step_keys = 256

    def block_parts(dx, h, order):
        logical = own_ref[req_at(0, dx)]
        group = logical // PER_GROUP
        base = (logical - group * PER_GROUP) * KB
        far = (P_SIZE - base + pslot).astype(F32) * (slopes[h] * LOG2E)
        tops = []
        for dz in order:
            m8 = None
            for c in range(KB // step_keys):
                keys = slice(c * step_keys, (c + 1) * step_keys)
                s = nt(kvb[dx, 0, h, keys, :], qz[dz, :, head(h)]) * (scale * LOG2E) + kbias[h, keys, :]
                sbuf[dz, keys, :] = s
                top = jnp.max(s.reshape(step_keys // 8, 8, ROWS), axis=0)
                m8 = top if m8 is None else jnp.maximum(m8, top)
            tops.append(jnp.max(m8, axis=0, keepdims=True))
        out = []
        for dz, m in zip(order, tops):
            l8, o = None, None
            for c in range(KB // step_keys):
                keys = slice(c * step_keys, (c + 1) * step_keys)
                w = jnp.exp2(sbuf[dz, keys, :] - m)
                low = jnp.sum(w.reshape(step_keys // 8, 8, ROWS), axis=0)
                t = nn(vt[:, keys], w.astype(BF16))
                l8, o = (low, t) if c == 0 else (l8 + low, o + t)
            valid = grp_ref[req_at(dz, 0)] == group
            out.append((jnp.where(valid, m - far, NEG), jnp.sum(l8, axis=0, keepdims=True), o))
        return out

    def held(dz, h):
        at = 4 * dz + 2 * h
        return accs[at : at + 1, :], accs[at + 1 : at + 2, :], acco[dz, h]

    def hold(dz, h, part):
        at = 4 * dz + 2 * h
        accs[at : at + 1, :] = part[0]
        accs[at + 1 : at + 2, :] = part[1]
        acco[dz, h] = part[2]

    for dx, h in ((0, 0), (0, 1), (1, 0), (3, 0), (1, 1), (3, 1), (2, 0), (2, 1)):
        if dx == 1:
            arrive_kv(1, 0, h)
        if dx == 3:
            arrive_kv(3, 1, h)
        if dx == 2:
            arrive_kv(2, 0, h)
            arrive_kv(2, 1, h)
        vt[...] = kvb[dx, 1, h].T
        rows = (2, 1, 3, 0)
        for dz, part in zip(rows, block_parts(dx, h, rows)):
            if dx != 0:
                part = combine([held(dz, h), part])
            if dx != 2 or dz == 0:
                hold(dz, h, part)
            else:
                zsend[dz - 1, h, 0:DH, :] = part[2].astype(BF16)
                zsend[dz - 1, h, DH:SLOT, :] = pack_stats(part[0], part[1])
                send(
                    zsend.at[dz - 1, h], zrecv.at[dz - 1, h], pzs.at[dz - 1, h], pzr.at[dz - 1, h], req_dev(dz, 0)
                )

    live = lax.broadcasted_iota(jnp.int32, (DH, ROWS), 1) < my_len
    for h in range(2):
        parts = [held(0, h), (sufs[2 * h : 2 * h + 1, :], sufs[2 * h + 1 : 2 * h + 2, :], sufo[h])]
        for dz in (1, 3, 2):
            arrive(zrecv.at[dz - 1, h], pzs.at[dz - 1, h], pzr.at[dz - 1, h])
            parts.append(read_slot(zrecv, (dz - 1, h)))
        m, l, o = combine(parts)
        att_out[:, head(h)] = jnp.where(live, o / l, 0.0).T.astype(BF16)

    loads["res"].wait()
    loads["ow"].wait()
    respad[...] = jnp.zeros_like(respad)
    respad[:, pl.ds(pl.multiple_of(core * COLS, COLS), COLS)] = res[...].astype(F32)
    wide = 512

    def head_term(half, n, rows):
        at = pl.multiple_of(half * HALF + n * wide, wide)
        t = nn(att_out[rows, :], ow[:, pl.ds(at, wide)])
        return t + jnp.where(half * (HALF // wide) + n == chip, respad[rows, :], 0.0)

    def rows_of(a):
        return slice(a * HR, (a + 1) * HR)

    for n in (0, 2, 1, 3):
        pre_s[n] = head_term(other, n, slice(None)).astype(BF16)
        send(pre_s.at[n], pre_r.at[n], p1s.at[n], p1r.at[n], partner)

    for a in range(2):
        for n in range(2):
            terms = []
            for cn in (n, n + 2):
                t = head_term(core, cn, rows_of(a))
                if a == 0:
                    arrive(pre_r.at[cn], p1s.at[cn], p1r.at[cn])
                terms.append(t + pre_r[cn, rows_of(a), :].astype(F32))
            for k in range(NCHIP):
                rs_s[a, k, :, n * wide : (n + 1) * wide] = jnp.concatenate(
                    [t[8 * k : 8 * k + 8] for t in terms], axis=0
                ).astype(BF16)
        for i, off in enumerate(CHIPS):
            send(rs_s.at[a, chip_at(off)], rs_r.at[a, i], r1s.at[a, i], r1r.at[a, i], chip_dev(off))
    loads["gain"].wait()
    gain_at = pl.multiple_of(core * HALF, HALF)
    gain_16 = jnp.concatenate(
        [
            jnp.broadcast_to(gain[0:1, pl.ds(gain_at, HALF // 2)], (8, HALF // 2)),
            jnp.broadcast_to(gain[0:1, pl.ds(gain_at + HALF // 2, HALF // 2)], (8, HALF // 2)),
        ],
        axis=0,
    )

    def both(v):
        return v[0:8] + v[8:16]

    def twice(v):
        return jnp.concatenate([v, v], axis=0)

    lane = lax.broadcasted_iota(jnp.int32, (8, 128), 1)
    for a in range(2):
        tot = rs_s[a, chip].astype(F32)
        for i in reversed(range(len(CHIPS))):
            arrive(rs_r.at[a, i], r1s.at[a, i], r1r.at[a, i])
            tot = tot + rs_r[a, i].astype(F32)
        mean_a = both(jnp.sum(tot, axis=1, keepdims=True)) * (1.0 / HALF)
        cent = tot - twice(mean_a)
        m2_a = both(jnp.sum(cent * cent, axis=1, keepdims=True))
        st_s[a] = jnp.where(lane < 64, mean_a, m2_a)
        send(st_s.at[a], st_r.at[a], sts.at[a], strv.at[a], partner)
        mixed[a, :, 0 : HALF // 2] = tot[0:8]
        mixed[a, :, HALF // 2 : HALF] = tot[8:16]
        arrive(st_r.at[a], sts.at[a], strv.at[a])
        mean_b, m2_b = st_r[a, :, 0:1], st_r[a, :, 64:65]
        diff = mean_a - mean_b
        mean = 0.5 * (mean_a + mean_b)
        var = (m2_a + m2_b + diff * diff * (HALF / 2)) * (1.0 / D)
        nall[a, core, chip] = ((tot - twice(mean)) * twice(lax.rsqrt(var + 1e-05)) * gain_16).astype(BF16)
        mine = nall.at[a, core, chip]
        for i, off in enumerate(CHIPS):
            send(mine, mine, ags.at[a, i], agr.at[a, i], chip_dev(off))
        send(mine, mine, fws.at[a, 7], fwr.at[a, 7], partner)

    def up_half(a, half):
        blocks = [nall[a, half, k].astype(F32) for k in range(NCHIP)]
        out = None
        for part in range(2):
            lhs = jnp.concatenate([v[8 * part : 8 * part + 8] for v in blocks], axis=0).astype(BF16)
            at = pl.multiple_of(half * HALF + part * (HALF // 2), HALF // 2)
            t = nn(lhs, uw[pl.ds(at, HALF // 2), :])
            out = t if out is None else out + t
        return out

    order = CHIPS + ((0, 0),)

    def unit_term(hid, a, off, which):
        block = chip_at(off) * 2 + which
        tmp[...] = nn(hid, dw[:, pl.ds(pl.multiple_of(block * COLS, COLS), COLS)])
        inner = lax.rem(block, NCHIP)
        add = mixed[a, :, pl.ds(pl.multiple_of(inner * COLS, COLS), COLS)]
        mine = pl.ds(pl.multiple_of(chip * 8, 8), 8)
        tmp[mine, :] = tmp[mine, :] + jnp.where(block // NCHIP == core, add, 0.0)
        return tmp[...]

    for a in range(2):
        for i in reversed(range(len(CHIPS))):
            src = nall.at[a, core, back(CHIPS[i])]
            arrive(src, ags.at[a, i], agr.at[a, i])
            send(src, src, fws.at[a, i], fwr.at[a, i], partner)
        if a == 0:
            loads["uw"].wait()
        acc = up_half(a, core)
        for i in range(len(CHIPS)):
            arrive(nall.at[a, other, back(CHIPS[i])], fws.at[a, i], fwr.at[a, i])
        arrive(nall.at[a, other, chip], fws.at[a, 7], fwr.at[a, 7])
        acc = acc + up_half(a, other)
        hid = (acc * (0.5 * (1.0 + erf(acc * (0.5**0.5))))).astype(BF16)
        if a == 0:
            loads["dw"].wait()
        for i, off in enumerate(order):
            pre2_s[a, i] = unit_term(hid, a, off, other).astype(BF16)
            send(pre2_s.at[a, i], pre2_r.at[a, i], p2s.at[a, i], p2r.at[a, i], partner)
        for i, off in enumerate(order):
            t = unit_term(hid, a, off, core)
            arrive(pre2_r.at[a, i], p2s.at[a, i], p2r.at[a, i])
            t = t + pre2_r[a, i].astype(F32)
            if i < len(CHIPS):
                rs2_s[a, i] = t.astype(BF16)
                send(rs2_s.at[a, i], rs2_r.at[a, i], r2s.at[a, i], r2r.at[a, i], chip_dev(off))
            else:
                outk[a] = t
    row_i = lax.broadcasted_iota(jnp.int32, (HR, COLS), 0)
    for a in range(2):
        out = outk[a]
        for i in reversed(range(len(CHIPS))):
            arrive(rs2_r.at[a, i], r2s.at[a, i], r2r.at[a, i])
            out = out + rs2_r[a, i].astype(F32)
        lay_out[rows_of(a), :] = jnp.where(row_i + a * HR < my_len, out, 0.0).astype(BF16)
    for cp in sends:
        cp.wait_send()


def shards(
    queries,
    suffix_kv,
    prefix_kv,
    resid,
    ln_gain,
    out_weight,
    up_weight,
    down_weight,
    lengths,
    req_group,
    prefix_owner,
):
    smem = pl.BlockSpec(memory_space=pltpu.SMEM)
    anym = pl.BlockSpec(memory_space=pl.ANY)
    vmem = pl.BlockSpec(memory_space=pltpu.VMEM)
    dma = pltpu.SemaphoreType.DMA
    vm = pltpu.VMEM
    n = HALF // 512
    nc = len(CHIPS)
    return pl.pallas_call(
        kernel,
        out_shape=[jax.ShapeDtypeStruct((ROWS, COLS), BF16)] * 2,
        in_specs=[smem] * 3 + [anym] * 8,
        out_specs=[vmem] * 2,
        scratch_shapes=[
            vm((NZH, ROWS, COLS), BF16),
            vm((2, S_MAX, COLS), BF16),
            vm((NX, 2, 2, KB, DH), BF16),
            vm((ROWS, COLS), BF16),
            vm((1, D), F32),
            vm((COLS, D), BF16),
            vm((D, UNITS), BF16),
            vm((UNITS, D), BF16),
            vm((DH, KB), BF16),
            vm((2, DH, ROWS), F32),
            vm((8, ROWS), F32),
            vm((2, KB, ROWS), F32),
            vm((NZH, KB, ROWS), F32),
            vm((NZH, 2, DH, ROWS), F32),
            vm((16, ROWS), F32),
            vm((3, 2, SLOT, ROWS), BF16),
            vm((3, 2, SLOT, ROWS), BF16),
            vm((ROWS, 512), F32),
            vm((n, ROWS, 512), BF16),
            vm((n, ROWS, 512), BF16),
            vm((2, NCHIP, 16, HALF // 2), BF16),
            vm((2, nc, 16, HALF // 2), BF16),
            vm((2, 8, 128), F32),
            vm((2, 8, 128), F32),
            vm((2, 8, HALF), F32),
            vm((2, 2, NCHIP, 16, HALF // 2), BF16),
            vm((HR, COLS), F32),
            vm((2, HR, COLS), F32),
            vm((2, 8, HR, COLS), BF16),
            vm((2, 8, HR, COLS), BF16),
            vm((2, nc, HR, COLS), BF16),
            vm((2, nc, HR, COLS), BF16),
            dma((11,)),
            dma((3,)),
            dma((3,)),
            dma((2, 2, 2)),
            dma((2, 2)),
            dma((NX, 2, 2)),
            dma((3, 2)),
            dma((3, 2)),
            dma((n,)),
            dma((n,)),
            dma((2, nc)),
            dma((2, nc)),
            dma((2,)),
            dma((2,)),
            dma((2, nc)),
            dma((2, nc)),
            dma((2, 8)),
            dma((2, 8)),
            dma((2, 8)),
            dma((2, 8)),
            dma((2, nc)),
            dma((2, nc)),
        ],
        compiler_params=pltpu.CompilerParams(
            collective_id=0, has_side_effects=True, vmem_limit_bytes=56 * 2**20
        ),
        name="prefill_layer",
    )(
        lengths,
        req_group,
        prefix_owner,
        queries,
        suffix_kv,
        prefix_kv,
        resid,
        ln_gain.reshape(1, D),
        out_weight,
        up_weight,
        down_weight,
    )


def solution(mesh):
    placed = (
        P("req", "mp"),
        P(None, "req", "mp"),
        P(None, "req", "mp"),
        P("req", "mp"),
        P(),
        P("mp", None),
        P(None, "mp"),
        P("mp", None),
        P(),
        P(),
        P(),
    )
    return jax.shard_map(
        shards,
        mesh=mesh,
        in_specs=placed,
        out_specs=(P("req", "mp"), P("req", "mp")),
        check_vma=False,
    )
```

```python
import functools

import jax
import jax.numpy as jnp
from jax import lax
from jax.experimental import pallas as pl
from jax.experimental.pallas import tpu as pltpu
from jax.sharding import PartitionSpec as P

MESH = pl.DeviceIdType.MESH
H = 32
DH = 128
KB = 512
S_MAX = 128
P_SIZE = 2048
PER_GROUP = P_SIZE // KB
NX = 4
NZH = 4
NY = 4
NZL = 2
NCHIP = NY * NZL
NREQ = NX * NZH
NEG = -1e30
ROWS = S_MAX
COLS = 2 * DH
D = 4096
HALF = D // 2
UNITS = 512
WIDE = 512
HR = ROWS // 2
STAT = 16
SLOT = DH + STAT
LOG2E = 1.4426950408889634

Z_FAR = (2, 1, 3)
CHIPS = ((1, 2), (1, 1), (1, 3), (0, 2), (1, 0), (0, 1), (0, 3))

F32 = jnp.float32
BF16 = jnp.bfloat16


def nt(a, b):
    return lax.dot_general(a, b, (((1,), (1,)), ((), ())), preferred_element_type=F32)


def nn(a, b):
    return lax.dot_general(a, b, (((1,), (0,)), ((), ())), preferred_element_type=F32)


def head(h):
    return slice(h * DH, (h + 1) * DH)


def slope_of(index):
    k = index + 1
    whole, part = k // 4, lax.rem(k, 4)
    out = jnp.float32(1.0)
    for i in range(1, 9):
        out = jnp.where(whole == i, jnp.float32(2.0**-i), out)
    frac = jnp.float32(1.0)
    for i in range(1, 4):
        frac = jnp.where(part == i, jnp.float32(2.0 ** (-0.25 * i)), frac)
    return out * frac


def split3(v):
    hi = v.astype(BF16).astype(F32)
    rest = v - hi
    mid = rest.astype(BF16).astype(F32)
    return hi, mid, rest - mid


def pack_stats(m, l):
    row = lax.broadcasted_iota(jnp.int32, (STAT, ROWS), 0)
    out = jnp.zeros((STAT, ROWS), F32)
    for at, part in enumerate(split3(m) + split3(l)):
        out = jnp.where(row == at, part, out)
    return out.astype(BF16)


def combine(parts):
    m = parts[0][0]
    for part in parts[1:]:
        m = jnp.maximum(m, part[0])
    l, o = None, None
    for part in parts:
        scale = jnp.exp2(part[0] - m)
        l = part[1] * scale if l is None else l + part[1] * scale
        o = part[2] * scale if o is None else o + part[2] * scale
    return m, l, o


def read_slot(ref, lead):
    st = ref[lead + (pl.ds(DH, STAT), slice(None))].astype(F32)
    m = st[0:1] + st[1:2] + st[2:3]
    l = st[3:4] + st[4:5] + st[5:6]
    return m, l, ref[lead + (pl.ds(0, DH), slice(None))].astype(F32)


def erf(x):
    return lax.erf(x)


def kernel(
    len_ref,
    grp_ref,
    own_ref,
    q_hbm,
    skv_hbm,
    pkv_hbm,
    res_hbm,
    gain_hbm,
    ow_hbm,
    uw_hbm,
    dw_hbm,
    att_out,
    lay_out,
    qz,
    skv,
    kvb,
    res,
    gain,
    ow,
    uw,
    dw,
    vt,
    sufo,
    sufs,
    kbias,
    sbuf,
    acco,
    accs,
    zsend,
    zrecv,
    respad,
    pre_s,
    pre_r,
    rs_s,
    rs_r,
    st_s,
    st_r,
    mixed,
    nall,
    outk,
    kept,
    pre2_s,
    pre2_r,
    rs2_s,
    rs2_r,
    loc,
    qzs,
    qzr,
    kvs,
    fks,
    kvr,
    pzs,
    pzr,
    p1s,
    p1r,
    r1s,
    r1r,
    sts,
    strv,
    ags,
    agr,
    fws,
    fwr,
    p2s,
    p2r,
    r2s,
    r2r,
):
    me_r = lax.axis_index("req")
    me_m = lax.axis_index("mp")
    zh, x = me_r // NX, lax.rem(me_r, NX)
    core = lax.rem(me_m, 2)
    chip = me_m // 2
    zl, y = chip // NY, lax.rem(chip, NY)
    other = 1 - core

    def req_at(dz, dx):
        return lax.rem(zh + dz, NZH) * NX + lax.rem(x + dx, NX)

    def req_dev(dz, dx):
        return (req_at(dz, dx), me_m)

    def chip_at(off):
        return lax.rem(zl + off[0], NZL) * NY + lax.rem(y + off[1], NY)

    def back(off):
        return lax.rem(zl + off[0], NZL) * NY + lax.rem(y + NY - off[1], NY)

    def chip_dev(off):
        return (me_r, chip_at(off) * 2 + core)

    partner = (me_r, chip * 2 + other)
    sends = []

    def send(src, dst, ssem, rsem, dev):
        cp = pltpu.make_async_remote_copy(
            src_ref=src, dst_ref=dst, send_sem=ssem, recv_sem=rsem, device_id=dev, device_id_type=MESH
        )
        cp.start()
        sends.append(cp)

    def flush(count):
        for _ in range(count):
            sends.pop(0).wait_send()

    def arrive(dst, ssem, rsem):
        pltpu.make_async_remote_copy(
            src_ref=dst, dst_ref=dst, send_sem=ssem, recv_sem=rsem, device_id=partner, device_id_type=MESH
        ).wait_recv()

    loads = {}
    for i, (name, src, dst) in enumerate(
        (
            ("q", q_hbm, qz.at[0]),
            ("skv", skv_hbm, skv),
            ("pkv00", pkv_hbm.at[0, :, head(0)], kvb.at[0, 0, 0]),
            ("pkv10", pkv_hbm.at[1, :, head(0)], kvb.at[0, 1, 0]),
            ("pkv01", pkv_hbm.at[0, :, head(1)], kvb.at[0, 0, 1]),
            ("pkv11", pkv_hbm.at[1, :, head(1)], kvb.at[0, 1, 1]),
            ("res", res_hbm, res),
            ("gain", gain_hbm, gain),
            *((f"ow{n}", ow_hbm.at[:, n * WIDE : (n + 1) * WIDE], ow.at[n]) for n in range(D // WIDE)),
            ("uw", uw_hbm, uw),
            *((f"dw{n}", dw_hbm.at[:, n * COLS : (n + 1) * COLS], dw.at[n]) for n in range(D // COLS)),
        )
    ):
        loads[name] = pltpu.make_async_copy(src, dst, loc.at[i])
        loads[name].start()

    barrier = pltpu.get_barrier_semaphore()
    peers = [req_dev(d, 0) for d in Z_FAR] + [req_dev(0, d) for d in (1, 3)]
    peers += [chip_dev(o) for o in CHIPS] + [partner]
    for dev in peers:
        pl.semaphore_signal(barrier, inc=1, device_id=dev, device_id_type=MESH)
    pl.semaphore_wait(barrier, len(peers))

    right, left = req_dev(0, 1), req_dev(0, 3)
    for i, d in enumerate(Z_FAR):
        send(q_hbm, qz.at[4 - d], qzs.at[d - 1], qzr.at[3 - d], req_dev(d, 0))
    for h in range(2):
        for first in range(2):
            k, v = first, 1 - first
            send(pkv_hbm.at[k, :, head(h)], kvb.at[3, k, h], kvs.at[0, k, h], kvr.at[3, k, h], right)
            send(pkv_hbm.at[v, :, head(h)], kvb.at[1, v, h], kvs.at[1, v, h], kvr.at[1, v, h], left)

    def arrive_kv(dx, part, h):
        arrive(kvb.at[dx, part, h], kvs.at[0, 0, 0], kvr.at[dx, part, h])

    my_len = len_ref[me_r]
    slopes = [slope_of(2 * me_m + h) for h in range(2)]
    scale = float(DH) ** (-0.5)
    loads["q"].wait()
    loads["skv"].wait()
    key_i = lax.broadcasted_iota(jnp.int32, (S_MAX, ROWS), 0)
    slot_i = lax.broadcasted_iota(jnp.int32, (S_MAX, ROWS), 1)
    allowed = (key_i <= slot_i) & (key_i < my_len)
    gap = (slot_i - key_i).astype(F32)
    pkey = lax.broadcasted_iota(jnp.int32, (KB, ROWS), 0).astype(F32)
    for h in range(2):
        s = (nt(skv[0, :, head(h)], qz[0, :, head(h)]) * scale - slopes[h] * gap) * LOG2E
        s = jnp.where(allowed, s, NEG)
        m = jnp.max(s, axis=0, keepdims=True)
        w = jnp.where(allowed, jnp.exp2(s - m), 0.0)
        sufs[2 * h : 2 * h + 1, :] = m
        sufs[2 * h + 1 : 2 * h + 2, :] = jnp.sum(w, axis=0, keepdims=True)
        sufo[h] = nn(skv[1, :, head(h)].T, w.astype(BF16))
        kbias[h] = pkey * (slopes[h] * LOG2E)

    for h in range(2):
        arrive_kv(3, 0, h)
        send(kvb.at[3, 0, h], kvb.at[2, 0, h], fks.at[0, h], kvr.at[2, 0, h], right)
        arrive_kv(1, 1, h)
        send(kvb.at[1, 1, h], kvb.at[2, 1, h], fks.at[1, h], kvr.at[2, 1, h], left)

    pslot = lax.broadcasted_iota(jnp.int32, (1, ROWS), 1)
    for name in ("pkv00", "pkv01", "pkv10", "pkv11"):
        loads[name].wait()
    for d in (1, 3, 2):
        arrive(qz.at[d], qzs.at[0], qzr.at[d - 1])
    step_keys = 256

    def block_parts(dx, h, order):
        logical = own_ref[req_at(0, dx)]
        group = logical // PER_GROUP
        base = (logical - group * PER_GROUP) * KB
        far = (P_SIZE - base + pslot).astype(F32) * (slopes[h] * LOG2E)
        tops = []
        for dz in order:
            m8 = None
            for c in range(KB // step_keys):
                keys = slice(c * step_keys, (c + 1) * step_keys)
                s = nt(kvb[dx, 0, h, keys, :], qz[dz, :, head(h)]) * (scale * LOG2E) + kbias[h, keys, :]
                sbuf[dz, keys, :] = s
                top = jnp.max(s.reshape(step_keys // 8, 8, ROWS), axis=0)
                m8 = top if m8 is None else jnp.maximum(m8, top)
            tops.append(jnp.max(m8, axis=0, keepdims=True))
        out = []
        for dz, m in zip(order, tops):
            l8, o = None, None
            for c in range(KB // step_keys):
                keys = slice(c * step_keys, (c + 1) * step_keys)
                w = jnp.exp2(sbuf[dz, keys, :] - m)
                low = jnp.sum(w.reshape(step_keys // 8, 8, ROWS), axis=0)
                t = nn(vt[:, keys], w.astype(BF16))
                l8, o = (low, t) if c == 0 else (l8 + low, o + t)
            valid = grp_ref[req_at(dz, 0)] == group
            out.append((jnp.where(valid, m - far, NEG), jnp.sum(l8, axis=0, keepdims=True), o))
        return out

    def held(dz, h):
        at = 4 * dz + 2 * h
        return accs[at : at + 1, :], accs[at + 1 : at + 2, :], acco[dz, h]

    def hold(dz, h, part):
        at = 4 * dz + 2 * h
        accs[at : at + 1, :] = part[0]
        accs[at + 1 : at + 2, :] = part[1]
        acco[dz, h] = part[2]

    for dx, h in ((0, 0), (0, 1), (1, 0), (3, 0), (1, 1), (3, 1), (2, 0), (2, 1)):
        if dx == 1:
            arrive_kv(1, 0, h)
        if dx == 3:
            arrive_kv(3, 1, h)
        if dx == 2:
            arrive_kv(2, 0, h)
            arrive_kv(2, 1, h)
        vt[...] = kvb[dx, 1, h].T
        rows = (2, 1, 3, 0)
        for dz, part in zip(rows, block_parts(dx, h, rows)):
            if dx != 0:
                part = combine([held(dz, h), part])
            if dx != 2 or dz == 0:
                hold(dz, h, part)
            else:
                zsend[dz - 1, h, 0:DH, :] = part[2].astype(BF16)
                zsend[dz - 1, h, DH:SLOT, :] = pack_stats(part[0], part[1])
                send(
                    zsend.at[dz - 1, h], zrecv.at[dz - 1, h], pzs.at[dz - 1, h], pzr.at[dz - 1, h], req_dev(dz, 0)
                )

    for name in loads:
        if name[:2] in ("ow", "uw", "dw", "re", "ga"):
            loads[name].wait()
    flush(len(sends) - 6)

    live = lax.broadcasted_iota(jnp.int32, (DH, ROWS), 1) < my_len
    for h in range(2):
        parts = [held(0, h), (sufs[2 * h : 2 * h + 1, :], sufs[2 * h + 1 : 2 * h + 2, :], sufo[h])]
        for dz in (1, 3, 2):
            arrive(zrecv.at[dz - 1, h], pzs.at[dz - 1, h], pzr.at[dz - 1, h])
            parts.append(read_slot(zrecv, (dz - 1, h)))
        m, l, o = combine(parts)
        att_out[:, head(h)] = jnp.where(live, o / l, 0.0).T.astype(BF16)

    respad[...] = jnp.zeros_like(respad)
    respad[:, pl.ds(pl.multiple_of(core * COLS, COLS), COLS)] = res[...].astype(F32)
    wide = WIDE

    def head_term(half, n, rows):
        block = half * (HALF // wide) + n
        return nn(att_out[rows, :], ow[block]) + jnp.where(block == chip, respad[rows, :], 0.0)

    def rows_of(a):
        return slice(a * HR, (a + 1) * HR)

    for n in (0, 2, 1, 3):
        pre_s[n] = head_term(other, n, slice(None)).astype(BF16)
        send(pre_s.at[n], pre_r.at[n], p1s.at[n], p1r.at[n], partner)

    for a in range(2):
        for n in range(2):
            terms = []
            for cn in (n, n + 2):
                t = head_term(core, cn, rows_of(a))
                if a == 0:
                    arrive(pre_r.at[cn], p1s.at[cn], p1r.at[cn])
                terms.append(t + pre_r[cn, rows_of(a), :].astype(F32))
            for k in range(NCHIP):
                rs_s[a, k, :, n * wide : (n + 1) * wide] = jnp.concatenate(
                    [t[8 * k : 8 * k + 8] for t in terms], axis=0
                ).astype(BF16)
        for i, off in enumerate(CHIPS):
            send(rs_s.at[a, chip_at(off)], rs_r.at[a, i], r1s.at[a, i], r1r.at[a, i], chip_dev(off))
    gain_at = pl.multiple_of(core * HALF, HALF)
    gain_16 = jnp.concatenate(
        [
            jnp.broadcast_to(gain[0:1, pl.ds(gain_at, HALF // 2)], (8, HALF // 2)),
            jnp.broadcast_to(gain[0:1, pl.ds(gain_at + HALF // 2, HALF // 2)], (8, HALF // 2)),
        ],
        axis=0,
    )

    def both(v):
        return v[0:8] + v[8:16]

    def twice(v):
        return jnp.concatenate([v, v], axis=0)

    lane = lax.broadcasted_iota(jnp.int32, (8, 128), 1)
    for a in range(2):
        tot = rs_s[a, chip].astype(F32)
        for i in reversed(range(len(CHIPS))):
            arrive(rs_r.at[a, i], r1s.at[a, i], r1r.at[a, i])
            tot = tot + rs_r[a, i].astype(F32)
        mean_a = both(jnp.sum(tot, axis=1, keepdims=True)) * (1.0 / HALF)
        cent = tot - twice(mean_a)
        m2_a = both(jnp.sum(cent * cent, axis=1, keepdims=True))
        st_s[a] = jnp.where(lane < 64, mean_a, m2_a)
        send(st_s.at[a], st_r.at[a], sts.at[a], strv.at[a], partner)
        mixed[a, :, 0 : HALF // 2] = tot[0:8]
        mixed[a, :, HALF // 2 : HALF] = tot[8:16]
        arrive(st_r.at[a], sts.at[a], strv.at[a])
        mean_b, m2_b = st_r[a, :, 0:1], st_r[a, :, 64:65]
        diff = mean_a - mean_b
        mean = 0.5 * (mean_a + mean_b)
        var = (m2_a + m2_b + diff * diff * (HALF / 2)) * (1.0 / D)
        nall[a, core, chip] = ((tot - twice(mean)) * twice(lax.rsqrt(var + 1e-05)) * gain_16).astype(BF16)
        mine = nall.at[a, core, chip]
        for i, off in enumerate(CHIPS):
            send(mine, mine, ags.at[a, i], agr.at[a, i], chip_dev(off))
        send(mine, mine, fws.at[a, 7], fwr.at[a, 7], partner)

    def up_half(a, half):
        blocks = [nall[a, half, k].astype(F32) for k in range(NCHIP)]
        out = None
        for part in range(2):
            lhs = jnp.concatenate([v[8 * part : 8 * part + 8] for v in blocks], axis=0).astype(BF16)
            at = pl.multiple_of(half * HALF + part * (HALF // 2), HALF // 2)
            t = nn(lhs, uw[pl.ds(at, HALF // 2), :])
            out = t if out is None else out + t
        return out

    order = CHIPS + ((0, 0),)

    my_block = lax.broadcasted_iota(jnp.int32, (HR, COLS), 0) // 8 == chip

    def unit_term(hid, a, off, which):
        block = chip_at(off) * 2 + which
        inner = lax.rem(block, NCHIP)
        add = mixed[a, :, pl.ds(pl.multiple_of(inner * COLS, COLS), COLS)]
        add = jnp.where(block // NCHIP == core, add, 0.0)
        return nn(hid, dw[block]) + jnp.where(my_block, jnp.concatenate([add] * (HR // 8), axis=0), 0.0)

    for a in range(2):
        for i in reversed(range(len(CHIPS))):
            src = nall.at[a, core, back(CHIPS[i])]
            arrive(src, ags.at[a, i], agr.at[a, i])
            send(src, src, fws.at[a, i], fwr.at[a, i], partner)
        acc = up_half(a, core)
        for i in range(len(CHIPS)):
            arrive(nall.at[a, other, back(CHIPS[i])], fws.at[a, i], fwr.at[a, i])
        arrive(nall.at[a, other, chip], fws.at[a, 7], fwr.at[a, 7])
        acc = acc + up_half(a, other)
        hid = (acc * (0.5 * (1.0 + erf(acc * (0.5**0.5))))).astype(BF16)
        for g in (0, 4):
            for i in range(g, g + 4):
                pre2_s[a, i] = unit_term(hid, a, order[i], other).astype(BF16)
            for i in range(g, g + 4):
                send(pre2_s.at[a, i], pre2_r.at[a, i], p2s.at[a, i], p2r.at[a, i], partner)
        for i, off in enumerate(order):
            outk[i] = unit_term(hid, a, off, core)
        for i, off in enumerate(order):
            arrive(pre2_r.at[a, i], p2s.at[a, i], p2r.at[a, i])
            t = outk[i] + pre2_r[a, i].astype(F32)
            if i < len(CHIPS):
                rs2_s[a, i] = t.astype(BF16)
                send(rs2_s.at[a, i], rs2_r.at[a, i], r2s.at[a, i], r2r.at[a, i], chip_dev(off))
            else:
                kept[a] = t
    flush(len(sends) - len(CHIPS))
    row_i = lax.broadcasted_iota(jnp.int32, (HR, COLS), 0)
    for a in range(2):
        out = kept[a]
        for i in reversed(range(len(CHIPS))):
            arrive(rs2_r.at[a, i], r2s.at[a, i], r2r.at[a, i])
            out = out + rs2_r[a, i].astype(F32)
        lay_out[rows_of(a), :] = jnp.where(row_i + a * HR < my_len, out, 0.0).astype(BF16)
    for cp in sends:
        cp.wait_send()


def hand_over(att_ref, lay_ref, att_out, lay_out):
    att_out[...] = att_ref[...]
    lay_out[...] = lay_ref[...]


def shards(
    queries,
    suffix_kv,
    prefix_kv,
    resid,
    ln_gain,
    out_weight,
    up_weight,
    down_weight,
    lengths,
    req_group,
    prefix_owner,
):
    smem = pl.BlockSpec(memory_space=pltpu.SMEM)
    anym = pl.BlockSpec(memory_space=pl.ANY)
    vmem = pl.BlockSpec(memory_space=pltpu.VMEM)
    dma = pltpu.SemaphoreType.DMA
    vm = pltpu.VMEM
    n = HALF // 512
    nc = len(CHIPS)
    results = pl.pallas_call(
        kernel,
        out_shape=[jax.ShapeDtypeStruct((ROWS, COLS), BF16)] * 2,
        in_specs=[smem] * 3 + [anym] * 8,
        out_specs=[vmem] * 2,
        scratch_shapes=[
            vm((NZH, ROWS, COLS), BF16),
            vm((2, S_MAX, COLS), BF16),
            vm((NX, 2, 2, KB, DH), BF16),
            vm((ROWS, COLS), BF16),
            vm((1, D), F32),
            vm((D // WIDE, COLS, WIDE), BF16),
            vm((D, UNITS), BF16),
            vm((D // COLS, UNITS, COLS), BF16),
            vm((DH, KB), BF16),
            vm((2, DH, ROWS), F32),
            vm((8, ROWS), F32),
            vm((2, KB, ROWS), F32),
            vm((NZH, KB, ROWS), F32),
            vm((NZH, 2, DH, ROWS), F32),
            vm((16, ROWS), F32),
            vm((3, 2, SLOT, ROWS), BF16),
            vm((3, 2, SLOT, ROWS), BF16),
            vm((ROWS, 512), F32),
            vm((n, ROWS, 512), BF16),
            vm((n, ROWS, 512), BF16),
            vm((2, NCHIP, 16, HALF // 2), BF16),
            vm((2, nc, 16, HALF // 2), BF16),
            vm((2, 8, 128), F32),
            vm((2, 8, 128), F32),
            vm((2, 8, HALF), F32),
            vm((2, 2, NCHIP, 16, HALF // 2), BF16),
            vm((8, HR, COLS), F32),
            vm((2, HR, COLS), F32),
            vm((2, 8, HR, COLS), BF16),
            vm((2, 8, HR, COLS), BF16),
            vm((2, nc, HR, COLS), BF16),
            vm((2, nc, HR, COLS), BF16),
            dma((40,)),
            dma((3,)),
            dma((3,)),
            dma((2, 2, 2)),
            dma((2, 2)),
            dma((NX, 2, 2)),
            dma((3, 2)),
            dma((3, 2)),
            dma((n,)),
            dma((n,)),
            dma((2, nc)),
            dma((2, nc)),
            dma((2,)),
            dma((2,)),
            dma((2, nc)),
            dma((2, nc)),
            dma((2, 8)),
            dma((2, 8)),
            dma((2, 8)),
            dma((2, 8)),
            dma((2, nc)),
            dma((2, nc)),
        ],
        compiler_params=pltpu.CompilerParams(
            collective_id=0, has_side_effects=True, vmem_limit_bytes=56 * 2**20
        ),
        name="prefill_layer",
    )(
        lengths,
        req_group,
        prefix_owner,
        queries,
        suffix_kv,
        prefix_kv,
        resid,
        ln_gain.reshape(1, D),
        out_weight,
        up_weight,
        down_weight,
    )
    return pl.pallas_call(
        hand_over,
        out_shape=[jax.ShapeDtypeStruct((ROWS, COLS), BF16)] * 2,
        in_specs=[vmem] * 2,
        out_specs=[vmem] * 2,
        name="hand_over",
    )(*results)


def solution(mesh):
    placed = (
        P("req", "mp"),
        P(None, "req", "mp"),
        P(None, "req", "mp"),
        P("req", "mp"),
        P(),
        P("mp", None),
        P(None, "mp"),
        P("mp", None),
        P(),
        P(),
        P(),
    )
    return jax.shard_map(
        shards,
        mesh=mesh,
        in_specs=placed,
        out_specs=(P("req", "mp"), P("req", "mp")),
        check_vma=False,
    )
```

```python
import functools

import jax
import jax.numpy as jnp
from jax import lax
from jax.experimental import pallas as pl
from jax.experimental.pallas import tpu as pltpu
from jax.sharding import PartitionSpec as P

MESH = pl.DeviceIdType.MESH
H = 32
DH = 128
KB = 512
S_MAX = 128
P_SIZE = 2048
PER_GROUP = P_SIZE // KB
NX = 4
NZH = 4
NY = 4
NZL = 2
NCHIP = NY * NZL
NREQ = NX * NZH
NEG = -1e30
ROWS = S_MAX
COLS = 2 * DH
D = 4096
HALF = D // 2
UNITS = 512
WIDE = 512
HR = ROWS // 2
STAT = 16
SLOT = DH + STAT
LOG2E = 1.4426950408889634

CHIPS = ((1, 2), (1, 1), (1, 3), (0, 2), (1, 0), (0, 1), (0, 3))

F32 = jnp.float32
BF16 = jnp.bfloat16


def nt(a, b):
    return lax.dot_general(a, b, (((1,), (1,)), ((), ())), preferred_element_type=F32)


def nn(a, b):
    return lax.dot_general(a, b, (((1,), (0,)), ((), ())), preferred_element_type=F32)


def head(h):
    return slice(h * DH, (h + 1) * DH)


def slope_of(index):
    k = index + 1
    whole, part = k // 4, lax.rem(k, 4)
    out = jnp.float32(1.0)
    for i in range(1, 9):
        out = jnp.where(whole == i, jnp.float32(2.0**-i), out)
    frac = jnp.float32(1.0)
    for i in range(1, 4):
        frac = jnp.where(part == i, jnp.float32(2.0 ** (-0.25 * i)), frac)
    return out * frac


def split3(v):
    hi = v.astype(BF16).astype(F32)
    rest = v - hi
    mid = rest.astype(BF16).astype(F32)
    return hi, mid, rest - mid


def pack_stats(m, l):
    row = lax.broadcasted_iota(jnp.int32, (STAT, ROWS), 0)
    out = jnp.zeros((STAT, ROWS), F32)
    for at, part in enumerate(split3(m) + split3(l)):
        out = jnp.where(row == at, part, out)
    return out.astype(BF16)


def combine(parts):
    m = parts[0][0]
    for part in parts[1:]:
        m = jnp.maximum(m, part[0])
    l, o = None, None
    for part in parts:
        scale = jnp.exp2(part[0] - m)
        l = part[1] * scale if l is None else l + part[1] * scale
        o = part[2] * scale if o is None else o + part[2] * scale
    return m, l, o


def read_slot(ref, lead):
    st = ref[lead + (pl.ds(DH, STAT), slice(None))].astype(F32)
    m = st[0:1] + st[1:2] + st[2:3]
    l = st[3:4] + st[4:5] + st[5:6]
    return m, l, ref[lead + (pl.ds(0, DH), slice(None))].astype(F32)


def erf(x):
    return lax.erf(x)


def kernel(
    len_ref,
    grp_ref,
    own_ref,
    q_hbm,
    skv_hbm,
    pkv_hbm,
    res_hbm,
    gain_hbm,
    ow_hbm,
    uw_hbm,
    dw_hbm,
    att_out,
    lay_out,
    qz,
    skv,
    kvb,
    res,
    gain,
    ow,
    uw,
    dw,
    vt,
    sufo,
    sufs,
    kbias,
    sbuf,
    acco,
    accs,
    zsend,
    zrecv,
    respad,
    pre_s,
    pre_r,
    rs_s,
    rs_r,
    st_s,
    st_r,
    mixed,
    nall,
    outk,
    kept,
    pre2_s,
    pre2_r,
    rs2_s,
    rs2_r,
    loc,
    seen_z,
    seen_mp,
    seen_far,
    qzs,
    qzr,
    kvs,
    fks,
    kvr,
    pzs,
    pzr,
    p1s,
    p1r,
    r1s,
    r1r,
    sts,
    strv,
    ags,
    agr,
    fws,
    fwr,
    p2s,
    p2r,
    r2s,
    r2r,
):
    me_r = lax.axis_index("req")
    me_m = lax.axis_index("mp")
    zh, x = me_r // NX, lax.rem(me_r, NX)
    core = lax.rem(me_m, 2)
    chip = me_m // 2
    zl, y = chip // NY, lax.rem(chip, NY)
    other = 1 - core

    def req_at(dz, dx):
        return lax.rem(zh + dz, NZH) * NX + lax.rem(x + dx, NX)

    def req_dev(dz, dx):
        return (req_at(dz, dx), me_m)

    def chip_at(off):
        return lax.rem(zl + off[0], NZL) * NY + lax.rem(y + off[1], NY)

    def back(off):
        return lax.rem(zl + off[0], NZL) * NY + lax.rem(y + NY - off[1], NY)

    def chip_dev(off):
        return (me_r, chip_at(off) * 2 + core)

    partner = (me_r, chip * 2 + other)

    def send(src, dst, ssem, rsem, dev):
        pltpu.make_async_remote_copy(
            src_ref=src, dst_ref=dst, send_sem=ssem, recv_sem=rsem, device_id=dev, device_id_type=MESH
        ).start()

    def both_ends(ref, ssem, rsem):
        return pltpu.make_async_remote_copy(
            src_ref=ref, dst_ref=ref, send_sem=ssem, recv_sem=rsem, device_id=partner, device_id_type=MESH
        )

    def arrive(ref, rsem):
        both_ends(ref, rsem, rsem).wait_recv()

    def sent(ref, ssem):
        both_ends(ref, ssem, ssem).wait_send()

    barrier = pltpu.get_barrier_semaphore()
    z_near = [req_dev(1, 0), req_dev(3, 0)]
    mp_near = [chip_dev((0, 1)), chip_dev((0, 3)), chip_dev((1, 0))]
    near = [req_dev(0, 1), req_dev(0, 3)] + z_near + mp_near + [partner]
    for dev in near:
        pl.semaphore_signal(barrier, inc=1, device_id=dev, device_id_type=MESH)

    loads = {
        "q": qz.at[0],
        "skv": skv,
        "pkv": kvb.at[0],
        "res": res,
        "gain": gain,
        "ow": ow,
        "uw": uw,
        "dw": dw,
    }
    pieces = [("q", q_hbm, qz.at[0]), ("skv", skv_hbm, skv)]
    pieces += [("pkv", pkv_hbm.at[p, :, head(h)], kvb.at[0, p, h]) for h in range(2) for p in range(2)]
    pieces += [("res", res_hbm, res), ("gain", gain_hbm, gain)]
    pieces += [("ow", ow_hbm.at[:, n * WIDE : (n + 1) * WIDE], ow.at[n]) for n in range(D // WIDE)]
    pieces += [("uw", uw_hbm, uw)]
    pieces += [("dw", dw_hbm.at[:, n * COLS : (n + 1) * COLS], dw.at[n]) for n in range(D // COLS)]
    names = list(loads)

    def load(wanted):
        for name, src, dst in pieces:
            if name in wanted:
                pltpu.make_async_copy(src, dst, loc.at[names.index(name)]).start()

    def loaded(name):
        pltpu.make_async_copy(loads[name], loads[name], loc.at[names.index(name)]).wait()

    load(("q", "skv", "pkv"))
    pl.semaphore_wait(barrier, len(near))

    right, left = req_dev(0, 1), req_dev(0, 3)
    for dev in z_near:
        pl.semaphore_signal(seen_z, inc=1, device_id=dev, device_id_type=MESH)
    for dev in mp_near:
        pl.semaphore_signal(seen_mp, inc=1, device_id=dev, device_id_type=MESH)
    for h in range(2):
        for first in range(2):
            k, v = first, 1 - first
            send(pkv_hbm.at[k, :, head(h)], kvb.at[3, k, h], kvs, kvr.at[2, k, h], right)
            send(pkv_hbm.at[v, :, head(h)], kvb.at[1, v, h], kvs, kvr.at[0, v, h], left)
        if h == 0:
            for d in (1, 3):
                send(q_hbm, qz.at[4 - d], qzs, qzr, req_dev(d, 0))
    pl.semaphore_wait(seen_z, 2)
    send(q_hbm, qz.at[2], qzs, qzr, req_dev(2, 0))
    load(("res", "gain", "ow", "uw", "dw"))

    def arrive_kv(dx, part, h):
        arrive(kvb.at[dx, part, h], kvr.at[dx - 1, part, h])

    my_len = len_ref[me_r]
    slopes = [slope_of(2 * me_m + h) for h in range(2)]
    scale = float(DH) ** (-0.5)
    loaded("q")
    loaded("skv")
    key_i = lax.broadcasted_iota(jnp.int32, (S_MAX, ROWS), 0)
    slot_i = lax.broadcasted_iota(jnp.int32, (S_MAX, ROWS), 1)
    allowed = (key_i <= slot_i) & (key_i < my_len)
    gap = (slot_i - key_i).astype(F32)
    pkey = lax.broadcasted_iota(jnp.int32, (KB, ROWS), 0).astype(F32)
    for h in range(2):
        s = (nt(skv[0, :, head(h)], qz[0, :, head(h)]) * scale - slopes[h] * gap) * LOG2E
        s = jnp.where(allowed, s, NEG)
        m = jnp.max(s, axis=0, keepdims=True)
        w = jnp.where(allowed, jnp.exp2(s - m), 0.0)
        sufs[2 * h : 2 * h + 1, :] = m
        sufs[2 * h + 1 : 2 * h + 2, :] = jnp.sum(w, axis=0, keepdims=True)
        sufo[h] = nn(skv[1, :, head(h)].T, w.astype(BF16))
        kbias[h] = pkey * (slopes[h] * LOG2E)

    for h in range(2):
        arrive_kv(3, 0, h)
        send(kvb.at[3, 0, h], kvb.at[2, 0, h], fks, kvr.at[1, 0, h], right)
        arrive_kv(1, 1, h)
        send(kvb.at[1, 1, h], kvb.at[2, 1, h], fks, kvr.at[1, 1, h], left)

    pslot = lax.broadcasted_iota(jnp.int32, (1, ROWS), 1)
    loaded("pkv")
    arrive(qz.at[pl.ds(1, 3)], qzr)
    step_keys = 256

    def block_parts(dx, h, order):
        logical = own_ref[req_at(0, dx)]
        group = logical // PER_GROUP
        base = (logical - group * PER_GROUP) * KB
        far = (P_SIZE - base + pslot).astype(F32) * (slopes[h] * LOG2E)
        tops = []
        for dz in order:
            m8 = None
            for c in range(KB // step_keys):
                keys = slice(c * step_keys, (c + 1) * step_keys)
                s = nt(kvb[dx, 0, h, keys, :], qz[dz, :, head(h)]) * (scale * LOG2E) + kbias[h, keys, :]
                sbuf[dz, keys, :] = s
                top = jnp.max(s.reshape(step_keys // 8, 8, ROWS), axis=0)
                m8 = top if m8 is None else jnp.maximum(m8, top)
            tops.append(jnp.max(m8, axis=0, keepdims=True))
        out = []
        for dz, m in zip(order, tops):
            l8, o = None, None
            for c in range(KB // step_keys):
                keys = slice(c * step_keys, (c + 1) * step_keys)
                w = jnp.exp2(sbuf[dz, keys, :] - m)
                low = jnp.sum(w.reshape(step_keys // 8, 8, ROWS), axis=0)
                t = nn(vt[:, keys], w.astype(BF16))
                l8, o = (low, t) if c == 0 else (l8 + low, o + t)
            valid = grp_ref[req_at(dz, 0)] == group
            out.append((jnp.where(valid, m - far, NEG), jnp.sum(l8, axis=0, keepdims=True), o))
        return out

    def held(dz, h):
        at = 4 * dz + 2 * h
        return accs[at : at + 1, :], accs[at + 1 : at + 2, :], acco[dz, h]

    def hold(dz, h, part):
        at = 4 * dz + 2 * h
        accs[at : at + 1, :] = part[0]
        accs[at + 1 : at + 2, :] = part[1]
        acco[dz, h] = part[2]

    for dx, h in ((0, 0), (0, 1), (1, 0), (3, 0), (1, 1), (3, 1), (2, 0), (2, 1)):
        if dx == 1:
            arrive_kv(1, 0, h)
        if dx == 3:
            arrive_kv(3, 1, h)
        if dx == 2:
            arrive_kv(2, 0, h)
            arrive_kv(2, 1, h)
        vt[...] = kvb[dx, 1, h].T
        rows = (2, 1, 3, 0)
        for dz, part in zip(rows, block_parts(dx, h, rows)):
            if dx != 0:
                part = combine([held(dz, h), part])
            if dx != 2 or dz == 0:
                hold(dz, h, part)
            else:
                zsend[h, dz - 1, 0:DH, :] = part[2].astype(BF16)
                zsend[h, dz - 1, DH:SLOT, :] = pack_stats(part[0], part[1])
                send(zsend.at[h, dz - 1], zrecv.at[h, dz - 1], pzs, pzr.at[h], req_dev(dz, 0))

    for name in ("res", "gain", "ow", "uw", "dw"):
        loaded(name)
    sent(qz.at[pl.ds(1, 3)], qzs)
    sent(kvb.at[pl.ds(0, 2)], kvs)
    sent(kvb.at[0], fks)
    pl.semaphore_wait(seen_mp, len(mp_near))
    pl.semaphore_signal(seen_far, inc=1, device_id=chip_dev((1, 0)), device_id_type=MESH)
    pl.semaphore_wait(seen_far, 1)

    live = lax.broadcasted_iota(jnp.int32, (DH, ROWS), 1) < my_len
    for h in range(2):
        parts = [held(0, h), (sufs[2 * h : 2 * h + 1, :], sufs[2 * h + 1 : 2 * h + 2, :], sufo[h])]
        arrive(zrecv.at[h], pzr.at[h])
        for dz in (1, 3, 2):
            parts.append(read_slot(zrecv, (h, dz - 1)))
        m, l, o = combine(parts)
        att_out[:, head(h)] = jnp.where(live, o / l, 0.0).T.astype(BF16)

    respad[...] = jnp.zeros_like(respad)
    respad[:, pl.ds(pl.multiple_of(core * COLS, COLS), COLS)] = res[...].astype(F32)
    wide = WIDE

    def head_term(half, n, rows):
        block = half * (HALF // wide) + n
        return nn(att_out[rows, :], ow[block]) + jnp.where(block == chip, respad[rows, :], 0.0)

    def rows_of(a):
        return slice(a * HR, (a + 1) * HR)

    for n in (0, 2, 1, 3):
        pre_s[n] = head_term(other, n, slice(None)).astype(BF16)
        send(pre_s.at[n], pre_r.at[n], p1s, p1r.at[n], partner)

    for a in range(2):
        for n in range(2):
            terms = []
            for cn in (n, n + 2):
                t = head_term(core, cn, rows_of(a))
                if a == 0:
                    arrive(pre_r.at[cn], p1r.at[cn])
                terms.append(t + pre_r[cn, rows_of(a), :].astype(F32))
            for k in range(NCHIP):
                rs_s[a, k, :, n * wide : (n + 1) * wide] = jnp.concatenate(
                    [t[8 * k : 8 * k + 8] for t in terms], axis=0
                ).astype(BF16)
        for i, off in enumerate(CHIPS):
            send(rs_s.at[a, chip_at(off)], rs_r.at[a, i], r1s, r1r.at[a], chip_dev(off))
    gain_at = pl.multiple_of(core * HALF, HALF)
    gain_16 = jnp.concatenate(
        [
            jnp.broadcast_to(gain[0:1, pl.ds(gain_at, HALF // 2)], (8, HALF // 2)),
            jnp.broadcast_to(gain[0:1, pl.ds(gain_at + HALF // 2, HALF // 2)], (8, HALF // 2)),
        ],
        axis=0,
    )

    def both(v):
        return v[0:8] + v[8:16]

    def twice(v):
        return jnp.concatenate([v, v], axis=0)

    lane = lax.broadcasted_iota(jnp.int32, (8, 128), 1)
    for a in range(2):
        tot = rs_s[a, chip].astype(F32)
        arrive(rs_r.at[a], r1r.at[a])
        for i in range(len(CHIPS)):
            tot = tot + rs_r[a, i].astype(F32)
        mean_a = both(jnp.sum(tot, axis=1, keepdims=True)) * (1.0 / HALF)
        cent = tot - twice(mean_a)
        m2_a = both(jnp.sum(cent * cent, axis=1, keepdims=True))
        st_s[a] = jnp.where(lane < 64, mean_a, m2_a)
        send(st_s.at[a], st_r.at[a], sts, strv.at[a], partner)
        mixed[a, :, 0 : HALF // 2] = tot[0:8]
        mixed[a, :, HALF // 2 : HALF] = tot[8:16]
        arrive(st_r.at[a], strv.at[a])
        mean_b, m2_b = st_r[a, :, 0:1], st_r[a, :, 64:65]
        diff = mean_a - mean_b
        mean = 0.5 * (mean_a + mean_b)
        var = (m2_a + m2_b + diff * diff * (HALF / 2)) * (1.0 / D)
        nall[a, core, chip] = ((tot - twice(mean)) * twice(lax.rsqrt(var + 1e-05)) * gain_16).astype(BF16)
        mine = nall.at[a, core, chip]
        for i, off in enumerate(CHIPS):
            send(mine, mine, ags, agr.at[a, i], chip_dev(off))
        send(mine, mine, fws, fwr.at[a], partner)

    def up_half(a, half):
        blocks = [nall[a, half, k].astype(F32) for k in range(NCHIP)]
        out = None
        for part in range(2):
            lhs = jnp.concatenate([v[8 * part : 8 * part + 8] for v in blocks], axis=0).astype(BF16)
            at = pl.multiple_of(half * HALF + part * (HALF // 2), HALF // 2)
            t = nn(lhs, uw[pl.ds(at, HALF // 2), :])
            out = t if out is None else out + t
        return out

    order = CHIPS + ((0, 0),)

    my_block = lax.broadcasted_iota(jnp.int32, (HR, COLS), 0) // 8 == chip

    def unit_term(hid, a, off, which):
        block = chip_at(off) * 2 + which
        inner = lax.rem(block, NCHIP)
        add = mixed[a, :, pl.ds(pl.multiple_of(inner * COLS, COLS), COLS)]
        add = jnp.where(block // NCHIP == core, add, 0.0)
        return nn(hid, dw[block]) + jnp.where(my_block, jnp.concatenate([add] * (HR // 8), axis=0), 0.0)

    for a in range(2):
        for i in reversed(range(len(CHIPS))):
            src = nall.at[a, core, back(CHIPS[i])]
            arrive(src, agr.at[a, i])
            send(src, src, fws, fwr.at[a], partner)
        acc = up_half(a, core)
        arrive(nall.at[a, other], fwr.at[a])
        acc = acc + up_half(a, other)
        hid = (acc * (0.5 * (1.0 + erf(acc * (0.5**0.5))))).astype(BF16)
        for g in (0, 4):
            for i in range(g, g + 4):
                pre2_s[a, i] = unit_term(hid, a, order[i], other).astype(BF16)
            for i in range(g, g + 4):
                send(pre2_s.at[a, i], pre2_r.at[a, i], p2s, p2r.at[a, g // 4], partner)
        for i, off in enumerate(order):
            outk[i] = unit_term(hid, a, off, core)
        for i, off in enumerate(order):
            if i % 4 == 0:
                arrive(pre2_r.at[a, pl.ds(i, 4)], p2r.at[a, i // 4])
            t = outk[i] + pre2_r[a, i].astype(F32)
            if i < len(CHIPS):
                rs2_s[a, i] = t.astype(BF16)
                send(rs2_s.at[a, i], rs2_r.at[a, i], r2s, r2r.at[a], chip_dev(off))
            else:
                kept[a] = t
    sent(zsend, pzs)
    sent(pre_s, p1s)
    sent(rs_r, r1s)
    sent(st_s, sts)
    sent(rs_r, ags)
    sent(nall.at[0], fws)
    sent(pre2_s, p2s)
    row_i = lax.broadcasted_iota(jnp.int32, (HR, COLS), 0)
    for a in range(2):
        out = kept[a]
        arrive(rs2_r.at[a], r2r.at[a])
        for i in range(len(CHIPS)):
            out = out + rs2_r[a, i].astype(F32)
        lay_out[rows_of(a), :] = jnp.where(row_i + a * HR < my_len, out, 0.0).astype(BF16)
    sent(rs2_s, r2s)


def hand_over(att_ref, lay_ref, att_out, lay_out):
    att_out[...] = att_ref[...]
    lay_out[...] = lay_ref[...]


def shards(
    queries,
    suffix_kv,
    prefix_kv,
    resid,
    ln_gain,
    out_weight,
    up_weight,
    down_weight,
    lengths,
    req_group,
    prefix_owner,
):
    smem = pl.BlockSpec(memory_space=pltpu.SMEM)
    anym = pl.BlockSpec(memory_space=pl.ANY)
    vmem = pl.BlockSpec(memory_space=pltpu.VMEM)
    dma = pltpu.SemaphoreType.DMA
    vm = pltpu.VMEM
    n = HALF // 512
    nc = len(CHIPS)
    results = pl.pallas_call(
        kernel,
        out_shape=[jax.ShapeDtypeStruct((ROWS, COLS), BF16)] * 2,
        in_specs=[smem] * 3 + [anym] * 8,
        out_specs=[vmem] * 2,
        scratch_shapes=[
            vm((NZH, ROWS, COLS), BF16),
            vm((2, S_MAX, COLS), BF16),
            vm((NX, 2, 2, KB, DH), BF16),
            vm((ROWS, COLS), BF16),
            vm((1, D), F32),
            vm((D // WIDE, COLS, WIDE), BF16),
            vm((D, UNITS), BF16),
            vm((D // COLS, UNITS, COLS), BF16),
            vm((DH, KB), BF16),
            vm((2, DH, ROWS), F32),
            vm((8, ROWS), F32),
            vm((2, KB, ROWS), F32),
            vm((NZH, KB, ROWS), F32),
            vm((NZH, 2, DH, ROWS), F32),
            vm((16, ROWS), F32),
            vm((2, 3, SLOT, ROWS), BF16),
            vm((2, 3, SLOT, ROWS), BF16),
            vm((ROWS, 512), F32),
            vm((n, ROWS, 512), BF16),
            vm((n, ROWS, 512), BF16),
            vm((2, NCHIP, 16, HALF // 2), BF16),
            vm((2, nc, 16, HALF // 2), BF16),
            vm((2, 8, 128), F32),
            vm((2, 8, 128), F32),
            vm((2, 8, HALF), F32),
            vm((2, 2, NCHIP, 16, HALF // 2), BF16),
            vm((8, HR, COLS), F32),
            vm((2, HR, COLS), F32),
            vm((2, 8, HR, COLS), BF16),
            vm((2, 8, HR, COLS), BF16),
            vm((2, nc, HR, COLS), BF16),
            vm((2, nc, HR, COLS), BF16),
            dma((8,)),
            pltpu.SemaphoreType.REGULAR,
            pltpu.SemaphoreType.REGULAR,
            pltpu.SemaphoreType.REGULAR,
            dma(()),
            dma(()),
            dma(()),
            dma(()),
            dma((NX - 1, 2, 2)),
            dma(()),
            dma((2,)),
            dma(()),
            dma((n,)),
            dma(()),
            dma((2,)),
            dma(()),
            dma((2,)),
            dma(()),
            dma((2, nc)),
            dma(()),
            dma((2,)),
            dma(()),
            dma((2, 2)),
            dma(()),
            dma((2,)),
        ],
        compiler_params=pltpu.CompilerParams(
            collective_id=0, has_side_effects=True, vmem_limit_bytes=56 * 2**20
        ),
        name="prefill_layer",
    )(
        lengths,
        req_group,
        prefix_owner,
        queries,
        suffix_kv,
        prefix_kv,
        resid,
        ln_gain.reshape(1, D),
        out_weight,
        up_weight,
        down_weight,
    )
    return pl.pallas_call(
        hand_over,
        out_shape=[jax.ShapeDtypeStruct((ROWS, COLS), BF16)] * 2,
        in_specs=[vmem] * 2,
        out_specs=[vmem] * 2,
        name="hand_over",
    )(*results)


def solution(mesh):
    placed = (
        P("req", "mp"),
        P(None, "req", "mp"),
        P(None, "req", "mp"),
        P("req", "mp"),
        P(),
        P("mp", None),
        P(None, "mp"),
        P("mp", None),
        P(),
        P(),
        P(),
    )
    return jax.shard_map(
        shards,
        mesh=mesh,
        in_specs=placed,
        out_specs=(P("req", "mp"), P("req", "mp")),
        check_vma=False,
    )
```
